1024 devices in a mesh: seq: 64 (over z, y_hi), chan: 16 (over y_lo, x, core).
Axes of the slice: x: 4, y: 4 (y_hi: 2, y_lo: 2; y = y_hi * 2 + y_lo), z: 32, core: 2. Of those that a mesh axis runs over, the one named last changes fastest.
Arguments:
- tokens: bfloat16 [16384, 4096], P('seq', 'chan'), may hold values from -6 to 6
- w_in: bfloat16 [4096, 3, 4096], P(None, None, 'chan'), may hold values from -0.09375 to 0.09375
- short_filter: float32 [3, 3, 4096], P(None, None, 'chan'), may hold values from -3 to 3
- mr_filter: bfloat16 [256, 128], P('chan'), may hold values from -0.5 to 0.5
- skip_gain: float32 [4096], P('chan'), may hold values from -4 to 4
- w_out: bfloat16 [4096, 4096], P('chan'), may hold values from -0.09375 to 0.09375
- segments: int32 [16384], replicated, may hold values from 0 to 15, never falling along the last dimension, each value on 1 to 2048 neighbouring positions
Outputs:
- mixed: bfloat16 [16384, 4096], P('seq', 'chan')
The draws below stay inside these ranges and needn't reach their ends.
Inputs may be any that keep to these rules, and one draw needn't show every extreme that they name: `segments`: document ids in contiguous sequence order never fall; each of the 16 documents holds 1 to 2048 positions and one holds exactly that many.
All inputs are finite; a program needn't handle non-finite values.
Results may differ from the reference program's by a relative error of at most 0.0076.
Values may be sent and summed in bfloat16 or wider, within the bound.
No kernel may reach another device: no remote copies, remote signals or barrier semaphores. Data moves between devices by JAX's collectives and lax.ppermute only.
A program may use at most 64 MiB of HBM per device.

```python
import math
import jax
import jax.numpy as jnp
import numpy as np
from jax import lax

D = 4096
GROUPS = 256
LEN = 128
SHORT = 3
DOCS = 16
TOKENS = 16384
GSIZE = 16
N_SEQ = 64


def steps_of(own_key, extent, cuts, smallest, high):
    loudness, own = 1.0, jax.random.fold_in(own_key, 6)
    for axis_at, shards_of in cuts:
        draws = jnp.exp(jax.random.uniform(jax.random.fold_in(own, axis_at), (shards_of,), jnp.float32, smallest / len(cuts), high / len(cuts)))
        loudness = loudness * jnp.repeat(draws, extent[axis_at] // shards_of).reshape([-1 if axis == axis_at else 1 for axis in range(len(extent))])
    return loudness


def profile(amount, total, bound, skew):
    loads = [(1 << 20) // math.isqrt(standing ** skew) + 1 for standing in range(2, amount + 1)]
    surplus, holding = total - bound - (amount - 1), [1] * (amount - 1)
    while surplus > 0:
        free = [i for i in range(amount - 1) if holding[i] < bound]
        whole, left = sum([loads[i] for i in free]), surplus
        for i in free:
            extra = min(bound - holding[i], max(1, left * loads[i] // whole), surplus)
            holding[i] = holding[i] + extra
            surplus = surplus - extra
    return np.array([bound] + holding)


def ragged(stream_key, count, total, bound, lean):
    if count == 2:
        one = jax.random.randint(stream_key, (), max(1, total - bound), min(bound, total - 1) + 1)
        return jnp.stack([one, total - one])
    lengths = jnp.asarray(profile(count, total, bound, lean), jnp.int32)
    pairs = (count - 1) // 2
    source_of, taker = lengths[1:1 + 2 * pairs:2], lengths[2:2 + 2 * pairs:2]
    slack = jnp.minimum(source_of - 1, bound - taker)
    passed = jax.random.randint(jax.random.fold_in(stream_key, 1), (pairs,), 0, 1 << 20) % (slack + 1)
    lengths = lengths.at[1:1 + 2 * pairs:2].set(source_of - passed).at[2:2 + 2 * pairs:2].set(taker + passed)
    return lengths[jax.random.permutation(jax.random.fold_in(stream_key, 2), count)]


def bell_draw(rng, dims, width, reach, shards=(), kind=jnp.bfloat16):
    result = jax.random.normal(rng, dims, jnp.float32) * width
    if len(shards) > 0:
        result = steps_of(rng, dims, shards, -0.22, 0.18) * result
    return jnp.clip(result, min=-reach, max=reach).astype(kind)


def setup_inputs(seed: int = 0) -> dict:
    streams_of = jax.random.split(jax.random.key(seed), 8)
    return {
        "tokens": bell_draw(streams_of[0], (TOKENS, D), 1.0, 6.0, ((0, 64), (1, 16))),
        "w_in": bell_draw(streams_of[1], (D, 3, D), D ** -0.5, 0.09375, ((2, 16),)),
        "short_filter": bell_draw(streams_of[2], (SHORT, 3, D), 0.6, 3.0, ((2, 16),), jnp.float32),
        "mr_filter": bell_draw(streams_of[3], (GROUPS, LEN), LEN ** -0.5, 0.5, ((0, 16),)),
        "skip_gain": bell_draw(streams_of[4], (D,), 1.0, 4.0, ((0, 16),), jnp.float32),
        "w_out": bell_draw(streams_of[5], (D, D), D ** -0.5, 0.09375, ((0, 16),)),
        "segments": jnp.searchsorted(jnp.cumsum(ragged(streams_of[6], DOCS, TOKENS, TOKENS // 8, 2)), jnp.arange(TOKENS), side="right").astype(jnp.int32),
    }


def unfold(folded):
    rest = folded.shape[1:]
    period_parts = folded.reshape((N_SEQ, TOKENS // (2 * N_SEQ), 2) + rest)
    first_slot = jnp.swapaxes(period_parts[:, :, 0], 0, 1)
    second = jnp.swapaxes(period_parts[::-1, :, 1], 0, 1)
    return jnp.concatenate([first_slot, second], axis=1).reshape((TOKENS,) + rest)


def refold(contiguous):
    rest = contiguous.shape[1:]
    period_parts = contiguous.reshape((TOKENS // (2 * N_SEQ), 2, N_SEQ) + rest)
    first_slot = period_parts[:, 0]
    second = period_parts[:, 1][:, ::-1]
    stacked = jnp.stack([first_slot, second], axis=2)
    return jnp.swapaxes(stacked, 0, 1).reshape((TOKENS,) + rest)


def short_conv(extended, seg_ext, weights):
    short_taps = weights.shape[0]
    row_count = extended.shape[0] - short_taps + 1
    seg_own = seg_ext[short_taps - 1:]
    tail_shape = (row_count,) + (1,) * (extended.ndim - 1)
    running = jnp.zeros((row_count,) + extended.shape[1:], jnp.float32)
    for tap_index in range(short_taps):
        lead_rows = short_taps - 1 - tap_index
        shifted = extended[lead_rows:lead_rows + row_count].astype(jnp.float32)
        same_doc = (seg_ext[lead_rows:lead_rows + row_count] == seg_own).astype(jnp.float32)
        running = running + weights[tap_index].astype(jnp.float32) * shifted * same_doc.reshape(tail_shape)
    return running


def band_matrix(filters):
    groups, tap_count = filters.shape
    flipped = filters[:, ::-1]
    blank = jnp.zeros((groups, tap_count), filters.dtype)
    row_pattern = jnp.concatenate([blank, flipped, blank], axis=1)
    tiled_rows = jnp.tile(row_pattern, (1, tap_count))
    tiled_rows = jnp.concatenate([tiled_rows, blank], axis=1)
    shaped = tiled_rows.reshape(groups, tap_count, 3 * tap_count + 1)[:, :, :2 * tap_count]
    return shaped[:, ::-1, :]


def long_conv(gated, band_mats, segments):
    tap_count = band_mats.shape[1]
    lead_block = jnp.zeros((tap_count,) + gated.shape[1:], gated.dtype)
    extended = jnp.concatenate([lead_block, gated])
    seg_ext = jnp.concatenate([jnp.full((tap_count,), -1, jnp.int32), segments])
    band_wide = band_mats.astype(jnp.float32)

    def one_block(block_index):
        offset = (block_index * tap_count).astype(jnp.int32)
        window = lax.dynamic_slice_in_dim(extended, offset, 2 * tap_count, 0).astype(jnp.float32)
        seg_window = lax.dynamic_slice_in_dim(seg_ext, offset, 2 * tap_count, 0)
        seg_own = lax.dynamic_slice_in_dim(seg_ext, offset + tap_count, tap_count, 0)
        doc_mask = seg_own[:, None] == seg_window[None, :]
        masked = jnp.where(doc_mask[None], band_wide, jnp.zeros((), band_wide.dtype))
        return jnp.einsum('gab,bgc->agc', masked, window)

    blocks_out = lax.map(one_block, jnp.arange(TOKENS // tap_count, dtype=jnp.int32))
    return blocks_out.reshape(gated.shape)


def reference(tokens, w_in, short_filter, mr_filter, skip_gain, w_out, segments):
    flat_in = w_in.reshape(D, 3 * D)
    projected = jnp.dot(tokens, flat_in, preferred_element_type=jnp.float32).astype(jnp.bfloat16)
    qkv = unfold(projected.reshape(TOKENS, 3, D))
    lead_rows = SHORT - 1
    extended = jnp.concatenate([jnp.zeros((lead_rows, 3, D), jnp.bfloat16), qkv])
    seg_ext = jnp.concatenate([jnp.full((lead_rows,), -1, jnp.int32), segments])
    convolved = short_conv(extended, seg_ext, short_filter)
    gated_in = (convolved[:, 1] * convolved[:, 2]).astype(jnp.bfloat16)
    band_mats = band_matrix(mr_filter)
    long_out = long_conv(gated_in.reshape(TOKENS, GROUPS, GSIZE), band_mats, segments).reshape(TOKENS, D)
    gated_out = (convolved[:, 0] * (long_out + skip_gain * gated_in.astype(jnp.float32))).astype(jnp.bfloat16)
    folded_out = refold(gated_out)
    return jnp.dot(folded_out, w_out, preferred_element_type=jnp.float32).astype(jnp.bfloat16)
```

```python
import functools

import jax
import jax.numpy as jnp
from jax import lax
from jax.experimental import pallas as pl
from jax.experimental.pallas import tpu as pltpu
from jax.sharding import PartitionSpec as P

BF16 = jnp.bfloat16
F32 = jnp.float32


def iota(shape, dim):
    return lax.broadcasted_iota(jnp.int32, shape, dim)


def dot(a, b):
    return jnp.dot(a, b, preferred_element_type=F32)


def cost(flops, moved):
    return pl.CostEstimate(flops=flops, bytes_accessed=moved, transcendentals=0)


def fold_source(position, seq_count):
    period, phase = position // (2 * seq_count), position % (2 * seq_count)
    late = phase >= seq_count
    device = jnp.where(late, 2 * seq_count - 1 - phase, phase)
    return device, 2 * period + late.astype(jnp.int32)


def unfold_kernel(seq_count, received, spread):
    copies, rows, lanes = spread.shape
    half = received.shape[1]
    device, slot = fold_source(iota((rows, received.shape[0]), 0), seq_count)
    column = iota((rows, received.shape[0]), 1)
    data = received[...]
    for part in range(lanes // half):
        pick = (column == device * 8 + part * 4 + slot).astype(BF16)
        moved = dot(pick, data).astype(BF16)
        for copy in range(copies):
            spread[copy, :, part * half : (part + 1) * half] = moved


def refold_kernel(seq_count, terms, outgoing):
    half = outgoing.shape[1]
    rows = terms.shape[1]
    total = terms[0].astype(F32)
    for term in range(1, terms.shape[0]):
        total = total + terms[term].astype(F32)
    mixed = total.astype(BF16)
    shape = (outgoing.shape[0], rows)
    device, slot = fold_source(iota(shape, 1), seq_count)
    target = iota(shape, 0)
    moved = None
    for part in range(terms.shape[2] // half):
        pick = (target == device * 8 + part * 4 + slot).astype(BF16)
        term = dot(pick, mixed[:, part * half : (part + 1) * half])
        moved = term if moved is None else moved + term
    outgoing[...] = moved.astype(BF16)


def project_first_kernel(core, rows, weights, total):
    @pl.when(pl.program_id(0) == 0)
    def _():
        total[...] = jnp.zeros_like(total)

    accumulate(rows, weights, total)


def accumulate(rows, weights, total):
    for block in range(rows.shape[0]):
        for part in range(total.shape[0]):
            total[part] += dot(rows[block], weights[part, block])


def segment_columns(segments, first, count):
    blocks = []
    for block in range(count):
        row = segments[pl.ds(first + block, 1), :].astype(F32)
        blocks.append(jnp.transpose(jnp.broadcast_to(row, (128, 128))))
    return jnp.concatenate(blocks, axis=0)


def short_conv(extended, columns, taps, lead):
    own = columns[lead:, :1]
    result = taps[0] * extended[lead:]
    for tap in range(1, taps.shape[0]):
        shifted = pltpu.roll(extended, tap, 0)[lead:]
        same = (pltpu.roll(columns, tap, 0)[lead:, :1] == own).astype(F32)
        result = result + taps[tap] * shifted * same
    return result


def project_last_kernel(scalars, rows, weights, partial, segments, short_filter, qkv, halo, total):
    step = pl.program_id(0)

    @pl.when(step == 0)
    def _():
        total[...] = partial[...]

    accumulate(rows, weights, total)

    @pl.when(step == pl.num_programs(0) - 1)
    def _():
        count = qkv.shape[1]
        for part in range(3):
            rounded = total[part].astype(BF16)
            qkv[part] = rounded
            halo[128 + 16 * part : 144 + 16 * part, :] = rounded[count - 16 :]
        columns = segment_columns(segments, 2 * scalars[1], 2)[count - 136 :]
        pair = []
        for part in (1, 2):
            extended = qkv[part].astype(F32)[count - 136 :]
            taps = jnp.stack([short_filter[tap, part : part + 1, :] for tap in range(3)])
            pair.append(short_conv(extended, columns, taps, 8))
        halo[:128, :] = (pair[0] * pair[1]).astype(BF16)


def band_kernel(filters, bands):
    groups, taps = filters.shape
    flip = iota((taps, 2 * taps), 1) == taps - iota((taps, 2 * taps), 0)
    first_rows = dot(filters[...], flip.astype(BF16))
    for group in range(groups):
        row = jnp.broadcast_to(first_rows[group : group + 1], (taps, 2 * taps))
        bands[group] = pltpu.roll(row, 0, 1, stride=1, stride_axis=0).astype(BF16)


def mix_kernel(scalars, qkv, halo, bands, segments, short_filter, skip_gain, gated_out):
    seq = scalars[1]
    count, chans = gated_out.shape
    groups = bands.shape[0]
    size = chans // groups
    ahead = segment_columns(segments, jnp.maximum(2 * seq - 1, 0), 1)
    ahead = jnp.where(seq > 0, ahead, -1.0)
    columns = jnp.concatenate([ahead, segment_columns(segments, 2 * seq, 2)], axis=0)
    convolved = []
    for part in range(3):
        lead = halo[128 + 16 * part : 144 + 16 * part, :].astype(F32)[8:]
        extended = jnp.concatenate([lead, qkv[part].astype(F32)], axis=0)
        taps = jnp.stack([short_filter[tap, part : part + 1, :] for tap in range(3)])
        convolved.append(short_conv(extended, columns[120:], taps, 8))
    gated = (convolved[1] * convolved[2]).astype(BF16)
    gated_ext = jnp.concatenate([halo[:128, :], gated], axis=0)
    lane_group = iota((256, 128), 1) // size
    for block in range(count // 128):
        own = columns[128 * (block + 1) : 128 * (block + 2)]
        masks = [
            (own == jnp.transpose(columns[128 * (block + k) : 128 * (block + k + 1)]))
            for k in range(2)
        ]
        mask = jnp.concatenate(masks, axis=1).astype(F32).astype(BF16)
        for side in range(chans // 128):
            lanes = slice(128 * side, 128 * (side + 1))
            window = gated_ext[128 * block : 128 * block + 256, lanes]
            total = jnp.zeros((128, 128), F32)
            for group in range(128 // size):
                band = bands[side * (128 // size) + group] * mask
                chosen = jnp.where(lane_group == group, window, jnp.zeros((), BF16))
                total = total + dot(band, chosen)
            rows = slice(128 * block, 128 * (block + 1))
            direct = skip_gain[:, lanes] * gated[rows, lanes].astype(F32)
            gated_out[rows, lanes] = (convolved[0][rows, lanes] * (total + direct)).astype(BF16)


def out_kernel(core, rows, weights, sums):
    sums[0] = dot(rows[...], weights[...]).astype(sums.dtype)


def whole(shape):
    return pl.BlockSpec(shape, lambda *_: (0,) * len(shape))


def body(tokens, w_in, short_filter, mr_filter, skip_gain, w_out, segments):
    rows, chans = tokens.shape
    width = w_in.shape[0]
    seq_count = lax.axis_size("seq")
    chan_count = lax.axis_size("chan")
    chips = chan_count // 2
    core = lax.axis_index("chan") % 2
    seq = lax.axis_index("seq")
    scalars = jnp.stack([core, seq]).astype(jnp.int32)
    same_core = [[2 * chip + c for chip in range(chips)] for c in range(2)]
    partners = [(i, i ^ 1) for i in range(chan_count)]
    segments = segments.reshape(-1, 128)
    gain = skip_gain.reshape(1, chans)
    half = chans // 2

    sendable = tokens.reshape(seq_count, 4, 2, half).swapaxes(1, 2).reshape(seq_count, 8, half)
    received = lax.all_to_all(sendable, "seq", 0, 0, tiled=True)
    spread = pl.pallas_call(
        functools.partial(unfold_kernel, seq_count),
        out_shape=jax.ShapeDtypeStruct((chips, rows, chans), BF16),
        cost_estimate=cost(4 * rows * rows * chans, 2 * (chips + 1) * rows * chans),
        name="unfold",
    )(received.reshape(seq_count * 8, half))
    near = lax.all_to_all(spread, "chan", 0, 0, axis_index_groups=same_core, tiled=True)
    far = lax.ppermute(near, "chan", partners)

    weights = w_in.transpose(1, 0, 2).reshape(3, chips, 2, chans, chans)
    project_cost = cost(3 * rows * width * chans, 3 * width * chans)
    steps = 4
    per = chips // steps
    rows_spec = pl.BlockSpec((per, rows, chans), lambda i, s: (i, 0, 0))
    total_spec = pl.BlockSpec((3, rows, chans), lambda i, s: (0, 0, 0))
    partial = pl.pallas_call(
        project_first_kernel,
        out_shape=jax.ShapeDtypeStruct((3, rows, chans), F32),
        grid_spec=pltpu.PrefetchScalarGridSpec(
            num_scalar_prefetch=1,
            grid=(steps,),
            in_specs=[
                rows_spec,
                pl.BlockSpec((3, per, None, chans, chans), lambda i, s: (0, i, s[0], 0, 0)),
            ],
            out_specs=total_spec,
        ),
        cost_estimate=project_cost,
        name="project_first",
    )(scalars, near, weights)
    bands = pl.pallas_call(
        band_kernel,
        out_shape=jax.ShapeDtypeStruct((mr_filter.shape[0], 128, 256), BF16),
        cost_estimate=cost(1 << 20, 1 << 21),
        name="bands",
    )(mr_filter)
    qkv, halo = pl.pallas_call(
        project_last_kernel,
        out_shape=(
            jax.ShapeDtypeStruct((3, rows, chans), BF16),
            jax.ShapeDtypeStruct((176, chans), BF16),
        ),
        grid_spec=pltpu.PrefetchScalarGridSpec(
            num_scalar_prefetch=1,
            grid=(steps,),
            in_specs=[
                rows_spec,
                pl.BlockSpec((3, per, None, chans, chans), lambda i, s: (0, i, 1 - s[0], 0, 0)),
                total_spec,
                whole(segments.shape),
                whole(short_filter.shape),
            ],
            out_specs=(total_spec, whole((176, chans))),
            scratch_shapes=[pltpu.VMEM((3, rows, chans), F32)],
        ),
        cost_estimate=project_cost,
        name="project_last",
    )(scalars, far, weights, partial, segments, short_filter)

    before = lax.ppermute(halo, "seq", [(i, i + 1) for i in range(seq_count - 1)])
    gated_out = pl.pallas_call(
        mix_kernel,
        out_shape=jax.ShapeDtypeStruct((rows, chans), BF16),
        grid_spec=pltpu.PrefetchScalarGridSpec(
            num_scalar_prefetch=1,
            grid=(1,),
            in_specs=[
                whole(qkv.shape),
                whole(before.shape),
                whole(bands.shape),
                whole(segments.shape),
                whole(short_filter.shape),
                whole(gain.shape),
            ],
            out_specs=whole((rows, chans)),
        ),
        cost_estimate=cost(1 << 29, 1 << 21),
        name="mix",
    )(scalars, qkv, before, bands, segments, short_filter, gain)

    def out_sums(other, dtype, name):
        return pl.pallas_call(
            out_kernel,
            out_shape=jax.ShapeDtypeStruct((chips, rows, chans), dtype),
            grid_spec=pltpu.PrefetchScalarGridSpec(
                num_scalar_prefetch=1,
                grid=(chips,),
                in_specs=[
                    whole((rows, chans)),
                    pl.BlockSpec(
                        (chans, chans), lambda i, s: (0, 2 * i + (1 - s[0] if other else s[0]))
                    ),
                ],
                out_specs=pl.BlockSpec((1, rows, chans), lambda i, s: (i, 0, 0)),
            ),
            cost_estimate=cost(rows * width * chans, width * chans),
            name=name,
        )(scalars, gated_out, w_out)

    given = lax.ppermute(out_sums(True, BF16, "out_other"), "chan", partners)
    kept = out_sums(False, F32, "out_own")
    pair = (kept + given.astype(F32)).astype(BF16)
    terms = lax.all_to_all(pair, "chan", 0, 0, axis_index_groups=same_core, tiled=True)
    outgoing = pl.pallas_call(
        functools.partial(refold_kernel, seq_count),
        out_shape=jax.ShapeDtypeStruct((seq_count * 8, half), BF16),
        cost_estimate=cost(4 * rows * rows * chans, 2 * (chips + 1) * rows * chans),
        name="refold",
    )(terms)
    returned = lax.all_to_all(outgoing.reshape(seq_count, 8, half), "seq", 0, 0, tiled=True)
    return returned.reshape(seq_count, 2, 4, half).swapaxes(1, 2).reshape(rows, chans)


def solution(mesh):
    return jax.shard_map(
        body,
        mesh=mesh,
        in_specs=(
            P("seq", "chan"),
            P(None, None, "chan"),
            P(None, None, "chan"),
            P("chan", None),
            P("chan"),
            P("chan", None),
            P(),
        ),
        out_specs=P("seq", "chan"),
        check_vma=False,
    )
```

```python
import functools

import jax
import jax.numpy as jnp
from jax import lax
from jax.experimental import pallas as pl
from jax.experimental.pallas import tpu as pltpu
from jax.sharding import PartitionSpec as P

BF16 = jnp.bfloat16
F32 = jnp.float32
SEQ = 64


def iota(shape, dim):
    return lax.broadcasted_iota(jnp.int32, shape, dim)


def dot(a, b):
    return jnp.dot(a, b, preferred_element_type=F32)


def cost(flops, moved):
    return pl.CostEstimate(flops=flops, bytes_accessed=moved, transcendentals=0)


def params(mib):
    return pltpu.CompilerParams(vmem_limit_bytes=mib << 20)


def block_of(device):
    z, half = device // 2, device % 2
    return jnp.where(half == 0, z, SEQ - 1 - z)


def fold_source(position):
    period, phase = position // (2 * SEQ), position % (2 * SEQ)
    late = phase >= SEQ
    return jnp.where(late, 2 * SEQ - 1 - phase, phase), 2 * period + late.astype(jnp.int32)


def pack_kernel(tokens, packed):
    shape = (packed.shape[0], tokens.shape[0])
    target, source = iota(shape, 0), iota(shape, 1)
    wanted = 4 * block_of(target // 8) + target % 4
    moved = None
    for part in range(2):
        pick = (source == wanted) & (target // 4 % 2 == part)
        term = dot(pick.astype(BF16), tokens[:, 128 * part : 128 * (part + 1)])
        moved = term if moved is None else moved + term
    packed[...] = moved.astype(BF16)


def unpack_kernel(packed, rows):
    shape = (rows.shape[0], packed.shape[0])
    target, source = iota(shape, 0), iota(shape, 1)
    for part in range(2):
        wanted = (block_of(source // 8) == target // 4) & (source % 8 == 4 * part + target % 4)
        moved = dot(wanted.astype(BF16), packed[...])
        rows[:, 128 * part : 128 * (part + 1)] = moved.astype(BF16)


def unfold_kernel(received, spread):
    copies, rows, _ = spread.shape
    shape = (rows, received.shape[0])
    device, slot = fold_source(iota(shape, 0))
    column = iota(shape, 1)
    for part in range(2):
        pick = (column == device * 8 + part * 4 + slot).astype(BF16)
        moved = dot(pick, received[...]).astype(BF16)
        for copy in range(copies):
            spread[copy, :, 128 * part : 128 * (part + 1)] = moved


def refold_kernel(terms, outgoing):
    total = terms[0].astype(F32)
    for term in range(1, terms.shape[0]):
        total = total + terms[term].astype(F32)
    mixed = total.astype(BF16)
    shape = (outgoing.shape[0], mixed.shape[0])
    device, slot = fold_source(iota(shape, 1))
    target = iota(shape, 0)
    moved = None
    for part in range(2):
        pick = (target == device * 8 + part * 4 + slot).astype(BF16)
        term = dot(pick, mixed[:, 128 * part : 128 * (part + 1)])
        moved = term if moved is None else moved + term
    outgoing[...] = moved.astype(BF16)


def segment_columns(segments, first, count):
    blocks = []
    for block in range(count):
        row = segments[pl.ds(first + block, 1), :].astype(F32)
        blocks.append(jnp.transpose(jnp.broadcast_to(row, (128, 128))))
    return jnp.concatenate(blocks, axis=0)


def short_conv(extended, columns, taps, lead):
    own = columns[lead:, :1]
    result = taps[0] * extended[lead:]
    for tap in range(1, taps.shape[0]):
        shifted = pltpu.roll(extended, tap, 0)[lead:]
        same = (pltpu.roll(columns, tap, 0)[lead:, :1] == own).astype(F32)
        result = result + taps[tap] * shifted * same
    return result


def project(other, rows, weights, fetched, sems, finish):
    chips, _, width = rows.shape
    core = lax.axis_index("chan") % 2
    parity = 1 - core if other else core
    copies = [
        pltpu.make_async_copy(weights.at[part, :, parity], fetched.at[part], sems.at[part])
        for part in range(3)
    ]
    for copy in copies:
        copy.start()
    data = jnp.concatenate([rows[chip] for chip in range(chips)], axis=1)
    for part in range(3):
        copies[part].wait()
        finish(part, dot(data, fetched[part].reshape(chips * width, width)))


def project_near_kernel(rows, weights, partial, fetched, sems):
    def finish(part, total):
        partial[part] = total

    project(False, rows, weights, fetched, sems, finish)


def project_far_kernel(rows, weights, partial, segments, short_filter, qkv, halo, fetched, sems):
    count = qkv.shape[1]

    def finish(part, total):
        rounded = (partial[part] + total).astype(BF16)
        qkv[part] = rounded
        halo[128 + 16 * part : 144 + 16 * part, :] = rounded[count - 16 :]

    project(True, rows, weights, fetched, sems, finish)
    block = block_of(lax.axis_index("seq"))
    columns = segment_columns(segments, 2 * block, 2)[count - 136 :]
    pair = []
    for part in (1, 2):
        extended = qkv[part].astype(F32)[count - 136 :]
        taps = jnp.stack([short_filter[tap, part : part + 1, :] for tap in range(3)])
        pair.append(short_conv(extended, columns, taps, 8))
    halo[:128, :] = (pair[0] * pair[1]).astype(BF16)


def band_kernel(filters, bands):
    groups, taps = filters.shape
    flip = iota((taps, 2 * taps), 1) == taps - iota((taps, 2 * taps), 0)
    first_rows = dot(filters[...], flip.astype(BF16))
    for group in range(groups):
        row = jnp.broadcast_to(first_rows[group : group + 1], (taps, 2 * taps))
        bands[group] = pltpu.roll(row, 0, 1, stride=1, stride_axis=0).astype(BF16)


def mix_kernel(qkv, halo, bands, segments, short_filter, skip_gain, gated_out):
    seq = block_of(lax.axis_index("seq"))
    count, chans = gated_out.shape
    groups = bands.shape[0]
    size = chans // groups
    ahead = segment_columns(segments, jnp.maximum(2 * seq - 1, 0), 1)
    ahead = jnp.where(seq > 0, ahead, -1.0)
    columns = jnp.concatenate([ahead, segment_columns(segments, 2 * seq, 2)], axis=0)
    convolved = []
    for part in range(3):
        lead = halo[128 + 16 * part : 144 + 16 * part, :].astype(F32)[8:]
        extended = jnp.concatenate([lead, qkv[part].astype(F32)], axis=0)
        taps = jnp.stack([short_filter[tap, part : part + 1, :] for tap in range(3)])
        convolved.append(short_conv(extended, columns[120:], taps, 8))
    gated = (convolved[1] * convolved[2]).astype(BF16)
    gated_ext = jnp.concatenate([halo[:128, :], gated], axis=0)
    lane_group = iota((256, 128), 1) // size
    for block in range(count // 128):
        own = columns[128 * (block + 1) : 128 * (block + 2)]
        masks = [
            (own == jnp.transpose(columns[128 * (block + k) : 128 * (block + k + 1)]))
            for k in range(2)
        ]
        mask = jnp.concatenate(masks, axis=1).astype(F32).astype(BF16)
        for side in range(chans // 128):
            lanes = slice(128 * side, 128 * (side + 1))
            window = gated_ext[128 * block : 128 * block + 256, lanes]
            total = jnp.zeros((128, 128), F32)
            for group in range(128 // size):
                band = bands[side * (128 // size) + group] * mask
                chosen = jnp.where(lane_group == group, window, jnp.zeros((), BF16))
                total = total + dot(band, chosen)
            rows = slice(128 * block, 128 * (block + 1))
            direct = skip_gain[:, lanes] * gated[rows, lanes].astype(F32)
            gated_out[rows, lanes] = (convolved[0][rows, lanes] * (total + direct)).astype(BF16)


def out_kernel(other, rows, weights, sums):
    core = lax.axis_index("chan") % 2
    parity = 1 - core if other else core
    chips, _, width = sums.shape
    for chip in range(chips):
        columns = pl.ds(pl.multiple_of((2 * chip + parity) * width, width), width)
        sums[chip] = dot(rows[...], weights[:, columns]).astype(sums.dtype)


def kernel(body, name, out_shape, mib, flops, moved, in_place=(), scratch=()):
    vector = pl.BlockSpec(memory_space=pltpu.VMEM)
    anywhere = pl.BlockSpec(memory_space=pltpu.HBM)

    def call(*args):
        return pl.pallas_call(
            body,
            out_shape=out_shape,
            in_specs=[anywhere if i in in_place else vector for i in range(len(args))],
            out_specs=jax.tree.map(lambda _: vector, out_shape),
            scratch_shapes=scratch,
            compiler_params=params(mib),
            cost_estimate=cost(flops, moved),
            name=name,
        )(*args)

    return call


def array(shape, dtype=BF16):
    return jax.ShapeDtypeStruct(shape, dtype)


def body(tokens, w_in, short_filter, mr_filter, skip_gain, w_out, segments):
    rows, chans = tokens.shape
    width = w_in.shape[0]
    chan_count = lax.axis_size("chan")
    chips = chan_count // 2
    same_core = [[2 * chip + c for chip in range(chips)] for c in range(2)]
    partners = [(i, i ^ 1) for i in range(chan_count)]
    holder = {int(k): d for d, k in enumerate([d // 2 if d % 2 == 0 else SEQ - 1 - d // 2 for d in range(SEQ)])}
    ahead = [(holder[k], holder[k + 1]) for k in range(SEQ - 1)]
    segments = segments.reshape(-1, 128)
    gain = skip_gain.reshape(1, chans)
    moved = rows * chans * 2

    packed = kernel(pack_kernel, "pack", array((8 * SEQ, 128)), 4, 1 << 26, 2 * moved)(tokens)
    received = lax.all_to_all(packed.reshape(SEQ, 8, 128), "seq", 0, 0, tiled=True)
    spread = kernel(unfold_kernel, "unfold", array((chips, rows, chans)), 8, 1 << 27, 9 * moved)(
        received.reshape(8 * SEQ, 128)
    )
    near = lax.all_to_all(spread, "chan", 0, 0, axis_index_groups=same_core, tiled=True)
    far = lax.ppermute(near, "chan", partners)
    bands = kernel(band_kernel, "bands", array((mr_filter.shape[0], 128, 256)), 8, 1 << 24, 8 * moved)(mr_filter)
    weights = w_in.transpose(1, 0, 2).reshape(3, chips, 2, chans, chans)
    work = 3 * rows * width * chans
    scratch = [pltpu.VMEM((3, chips, chans, chans), BF16), pltpu.SemaphoreType.DMA((3,))]
    partial = kernel(
        project_near_kernel, "project_near", array((3, rows, chans), F32), 51, work, 40 * moved, (1,), scratch
    )(near, weights)
    qkv, halo = kernel(
        project_far_kernel,
        "project_far",
        (array((3, rows, chans)), array((176, chans))),
        51,
        work,
        40 * moved,
        (1,),
        scratch,
    )(far, weights, partial, segments, short_filter)

    before = lax.ppermute(halo, "seq", ahead)
    gated_out = kernel(mix_kernel, "mix", array((rows, chans)), 8, 1 << 29, 16 * moved)(
        qkv, before, bands, segments, short_filter, gain
    )

    def out_sums(other, dtype, name):
        return kernel(
            functools.partial(out_kernel, other),
            name,
            array((chips, rows, chans), dtype),
            8,
            rows * width * chans,
            16 * moved,
        )(gated_out, w_out)

    given = lax.ppermute(out_sums(True, BF16, "out_other"), "chan", partners)
    kept = out_sums(False, F32, "out_own")
    pair = (kept + given.astype(F32)).astype(BF16)
    terms = lax.all_to_all(pair, "chan", 0, 0, axis_index_groups=same_core, tiled=True)
    outgoing = kernel(refold_kernel, "refold", array((8 * SEQ, 128)), 8, 1 << 27, 9 * moved)(terms)
    returned = lax.all_to_all(outgoing.reshape(SEQ, 8, 128), "seq", 0, 0, tiled=True)
    return kernel(unpack_kernel, "unpack", array((rows, chans)), 4, 1 << 27, 2 * moved)(
        returned.reshape(8 * SEQ, 128)
    )


def solution(mesh):
    return jax.shard_map(
        body,
        mesh=mesh,
        in_specs=(
            P("seq", "chan"),
            P(None, None, "chan"),
            P(None, None, "chan"),
            P("chan", None),
            P("chan"),
            P("chan", None),
            P(),
        ),
        out_specs=P("seq", "chan"),
        check_vma=False,
    )
```

```python
import jax
import jax.numpy as jnp
from jax import lax
from jax.experimental import pallas as pl
from jax.experimental.pallas import tpu as pltpu
from jax.sharding import PartitionSpec as P

BF16 = jnp.bfloat16
F32 = jnp.float32
SEQ = 64


def iota(shape, dim):
    return lax.broadcasted_iota(jnp.int32, shape, dim)


def dot(a, b):
    return jnp.dot(a, b, preferred_element_type=F32)


def cost(flops, moved):
    return pl.CostEstimate(flops=flops, bytes_accessed=moved, transcendentals=0)


def params(mib):
    return pltpu.CompilerParams(vmem_limit_bytes=mib << 20)


def block_of(device):
    z, half = device // 2, device % 2
    return jnp.where(half == 0, z, SEQ - 1 - z)


def fold_source(position):
    period, phase = position // (2 * SEQ), position % (2 * SEQ)
    late = phase >= SEQ
    return jnp.where(late, 2 * SEQ - 1 - phase, phase), 2 * period + late.astype(jnp.int32)


def pack_kernel(tokens, packed):
    shape = (packed.shape[0], tokens.shape[0])
    target, source = iota(shape, 0), iota(shape, 1)
    wanted = 4 * block_of(target // 8) + target % 4
    moved = None
    for part in range(2):
        pick = (source == wanted) & (target // 4 % 2 == part)
        term = dot(pick.astype(BF16), tokens[:, 128 * part : 128 * (part + 1)])
        moved = term if moved is None else moved + term
    packed[...] = moved.astype(BF16)


def unpack(packed, count):
    shape = (count, packed.shape[0])
    target, source = iota(shape, 0), iota(shape, 1)
    mine = block_of(source // 8) == target // 4
    halves = []
    for part in range(2):
        pick = mine & (source % 8 == 4 * part + target % 4)
        halves.append(dot(pick.astype(BF16), packed[...]).astype(BF16))
    return jnp.concatenate(halves, axis=1)


def unfold_kernel(received, spread):
    copies, rows, _ = spread.shape
    shape = (rows, received.shape[0])
    device, slot = fold_source(iota(shape, 0))
    column = iota(shape, 1)
    for part in range(2):
        pick = (column == device * 8 + part * 4 + slot).astype(BF16)
        moved = dot(pick, received[...]).astype(BF16)
        for copy in range(copies):
            spread[copy, :, 128 * part : 128 * (part + 1)] = moved


def refold(gated, outgoing):
    shape = (outgoing.shape[0], gated.shape[0])
    device, slot = fold_source(iota(shape, 1))
    target = iota(shape, 0)
    moved = None
    for part in range(2):
        pick = (target == device * 8 + part * 4 + slot).astype(BF16)
        term = dot(pick, gated[:, 128 * part : 128 * (part + 1)])
        moved = term if moved is None else moved + term
    outgoing[...] = moved.astype(BF16)


def sum_kernel(terms, mixed):
    total = terms[0].astype(F32)
    for term in range(1, terms.shape[0]):
        total = total + terms[term].astype(F32)
    mixed[...] = total.astype(BF16)


def segment_columns(segments, first, count):
    blocks = []
    for block in range(count):
        row = segments[pl.ds(first + block, 1), :].astype(F32)
        blocks.append(jnp.transpose(jnp.broadcast_to(row, (128, 128))))
    return jnp.concatenate(blocks, axis=0)


def short_conv(extended, columns, taps, lead):
    own = columns[lead:, :1]
    result = taps[0] * extended[lead:]
    for tap in range(1, taps.shape[0]):
        shifted = pltpu.roll(extended, tap, 0)[lead:]
        same = (pltpu.roll(columns, tap, 0)[lead:, :1] == own).astype(F32)
        result = result + taps[tap] * shifted * same
    return result


def join(blocks):
    return jnp.concatenate([blocks[chip] for chip in range(blocks.shape[0])], axis=1)


def project_near_kernel(rows, weights, partial, far_lines, lines, sems):
    core = lax.axis_index("chan") % 2
    chips, _, width = rows.shape
    copies = [
        pltpu.make_async_copy(weights.at[part, :, core], lines.at[part], sems.at[part])
        for part in range(3)
    ]
    copies.append(pltpu.make_async_copy(weights.at[:, :, 1 - core], far_lines, sems.at[3]))
    for copy in copies:
        copy.start()
    data = join(rows)
    for part in range(3):
        copies[part].wait()
        partial[part] = dot(data, lines[part].reshape(chips * width, width))
    copies[3].wait()


def project_far_kernel(rows, lines, partial, segments, short_filter, qkv, halo):
    chips, count, width = rows.shape
    data = join(rows)
    for part in range(3):
        total = partial[part] + dot(data, lines[part].reshape(chips * width, width))
        rounded = total.astype(BF16)
        qkv[part] = rounded
        halo[128 + 16 * part : 144 + 16 * part, :] = rounded[count - 16 :]
    block = block_of(lax.axis_index("seq"))
    columns = segment_columns(segments, 2 * block, 2)[count - 136 :]
    pair = []
    for part in (1, 2):
        extended = qkv[part].astype(F32)[count - 136 :]
        taps = jnp.stack([short_filter[tap, part : part + 1, :] for tap in range(3)])
        pair.append(short_conv(extended, columns, taps, 8))
    halo[:128, :] = (pair[0] * pair[1]).astype(BF16)


def band_kernel(filters, bands):
    groups, taps = filters.shape
    flip = iota((taps, 2 * taps), 1) == taps - iota((taps, 2 * taps), 0)
    first_rows = dot(filters[...], flip.astype(BF16))
    for group in range(groups):
        row = jnp.broadcast_to(first_rows[group : group + 1], (taps, 2 * taps))
        bands[group] = pltpu.roll(row, 0, 1, stride=1, stride_axis=0).astype(BF16)


def mix_kernel(qkv, halo, bands, segments, short_filter, skip_gain, outgoing, gated_out):
    seq = block_of(lax.axis_index("seq"))
    count, chans = gated_out.shape
    groups = bands.shape[0]
    size = chans // groups
    ahead = segment_columns(segments, jnp.maximum(2 * seq - 1, 0), 1)
    ahead = jnp.where(seq > 0, ahead, -1.0)
    columns = jnp.concatenate([ahead, segment_columns(segments, 2 * seq, 2)], axis=0)
    convolved = []
    for part in range(3):
        lead = halo[128 + 16 * part : 144 + 16 * part, :].astype(F32)[8:]
        extended = jnp.concatenate([lead, qkv[part].astype(F32)], axis=0)
        taps = jnp.stack([short_filter[tap, part : part + 1, :] for tap in range(3)])
        convolved.append(short_conv(extended, columns[120:], taps, 8))
    gated = (convolved[1] * convolved[2]).astype(BF16)
    gated_ext = jnp.concatenate([halo[:128, :], gated], axis=0)
    lane_group = iota((256, 128), 1) // size
    for block in range(count // 128):
        own = columns[128 * (block + 1) : 128 * (block + 2)]
        masks = [
            (own == jnp.transpose(columns[128 * (block + k) : 128 * (block + k + 1)]))
            for k in range(2)
        ]
        mask = jnp.concatenate(masks, axis=1).astype(F32).astype(BF16)
        for side in range(chans // 128):
            lanes = slice(128 * side, 128 * (side + 1))
            window = gated_ext[128 * block : 128 * block + 256, lanes]
            total = jnp.zeros((128, 128), F32)
            for group in range(128 // size):
                band = bands[side * (128 // size) + group] * mask
                chosen = jnp.where(lane_group == group, window, jnp.zeros((), BF16))
                total = total + dot(band, chosen)
            rows = slice(128 * block, 128 * (block + 1))
            direct = skip_gain[:, lanes] * gated[rows, lanes].astype(F32)
            gated_out[rows, lanes] = (convolved[0][rows, lanes] * (total + direct)).astype(BF16)
    refold(gated_out, outgoing)


def pick_kernel(weights, given, kept, sems):
    core = lax.axis_index("chan") % 2
    copies = []
    for i, (lines, parity) in enumerate(((given, 1 - core), (kept, core))):
        chips, _, width = lines.shape
        for chip in range(chips):
            columns = pl.ds(pl.multiple_of((2 * chip + parity) * width, width), width)
            copies.append(pltpu.make_async_copy(weights.at[:, columns], lines.at[chip], sems.at[i, chip]))
    for copy in copies:
        copy.start()
    for copy in copies:
        copy.wait()


def out_near_kernel(packed, lines, sums):
    rows = unpack(packed, sums.shape[1])
    for chip in range(sums.shape[0]):
        sums[chip] = dot(rows, lines[chip])


def out_far_kernel(packed, lines, near, sums):
    rows = unpack(packed, sums.shape[1])
    for chip in range(sums.shape[0]):
        sums[chip] = (near[chip] + dot(rows, lines[chip])).astype(BF16)


def kernel(body, name, out_shape, mib, flops, moved, in_place=(), scratch=()):
    vector = pl.BlockSpec(memory_space=pltpu.VMEM)
    anywhere = pl.BlockSpec(memory_space=pltpu.HBM)

    def call(*args):
        return pl.pallas_call(
            body,
            out_shape=out_shape,
            in_specs=[anywhere if i in in_place else vector for i in range(len(args))],
            out_specs=jax.tree.map(lambda _: vector, out_shape),
            scratch_shapes=scratch,
            compiler_params=params(mib),
            cost_estimate=cost(flops, moved),
            name=name,
        )(*args)

    return call


def array(shape, dtype=BF16):
    return jax.ShapeDtypeStruct(shape, dtype)


def over_seq(packed):
    chunks = packed.reshape(SEQ, 8, 128)
    return lax.all_to_all(chunks, "seq", 0, 0, tiled=True).reshape(8 * SEQ, 128)


def body(tokens, w_in, short_filter, mr_filter, skip_gain, w_out, segments):
    rows, chans = tokens.shape
    width = w_in.shape[0]
    chan_count = lax.axis_size("chan")
    chips = chan_count // 2
    same_core = [[2 * chip + c for chip in range(chips)] for c in range(2)]
    partners = [(i, i ^ 1) for i in range(chan_count)]
    holder = {int(k): d for d, k in enumerate([d // 2 if d % 2 == 0 else SEQ - 1 - d // 2 for d in range(SEQ)])}
    ahead = [(holder[k], holder[k + 1]) for k in range(SEQ - 1)]
    segments = segments.reshape(-1, 128)
    gain = skip_gain.reshape(1, chans)
    moved = rows * chans * 2

    packed = kernel(pack_kernel, "pack", array((8 * SEQ, 128)), 4, 1 << 26, 2 * moved)(tokens)
    spread = kernel(unfold_kernel, "unfold", array((chips, rows, chans)), 8, 1 << 27, 9 * moved)(over_seq(packed))
    near = lax.all_to_all(spread, "chan", 0, 0, axis_index_groups=same_core, tiled=True)
    far = lax.ppermute(near, "chan", partners)
    bands = kernel(band_kernel, "bands", array((mr_filter.shape[0], 128, 256)), 8, 1 << 24, 8 * moved)(mr_filter)
    weights = w_in.transpose(1, 0, 2).reshape(3, chips, 2, chans, chans)
    lines = (3, chips, chans, chans)
    work = 3 * rows * width * chans
    partial, far_lines = kernel(
        project_near_kernel,
        "project_near",
        (array((3, rows, chans), F32), array(lines)),
        47,
        work,
        60 * moved,
        (1,),
        [pltpu.VMEM(lines, BF16), pltpu.SemaphoreType.DMA((4,))],
    )(near, weights)
    qkv, halo = kernel(
        project_far_kernel,
        "project_far",
        (array((3, rows, chans)), array((176, chans))),
        8,
        work,
        40 * moved,
    )(far, far_lines, partial, segments, short_filter)

    before = lax.ppermute(halo, "seq", ahead)
    block = array((chips, rows, chans))
    given, kept = kernel(
        pick_kernel, "pick", (block, block), 8, 0, 32 * moved, (0,), [pltpu.SemaphoreType.DMA((2, chips))]
    )(w_out)
    taken = lax.ppermute(given, "chan", partners)
    outgoing = kernel(
        mix_kernel, "mix", array((8 * SEQ, 128)), 8, 1 << 29, 16 * moved, (), [pltpu.VMEM((rows, chans), BF16)]
    )(qkv, before, bands, segments, short_filter, gain)
    returned = over_seq(outgoing)
    other = lax.ppermute(returned, "chan", partners)
    sums = kernel(out_near_kernel, "out_near", array(block.shape, F32), 8, work // 3, 16 * moved)(returned, kept)
    sums = kernel(out_far_kernel, "out_far", block, 8, work // 3, 16 * moved)(other, taken, sums)
    terms = lax.all_to_all(sums, "chan", 0, 0, axis_index_groups=same_core, tiled=True)
    return kernel(sum_kernel, "sum", array((rows, chans)), 4, 1 << 20, 9 * moved)(terms)


def solution(mesh):
    return jax.shard_map(
        body,
        mesh=mesh,
        in_specs=(
            P("seq", "chan"),
            P(None, None, "chan"),
            P(None, None, "chan"),
            P("chan", None),
            P("chan"),
            P("chan", None),
            P(),
        ),
        out_specs=P("seq", "chan"),
        check_vma=False,
    )
```

```python
import jax
import jax.numpy as jnp
from jax import lax
from jax.experimental import pallas as pl
from jax.experimental.pallas import tpu as pltpu
from jax.sharding import PartitionSpec as P

BF16 = jnp.bfloat16
F32 = jnp.float32
SEQ = 64


def iota(shape, dim):
    return lax.broadcasted_iota(jnp.int32, shape, dim)


def dot(a, b):
    return jnp.dot(a, b, preferred_element_type=F32)


def cost(flops, moved):
    return pl.CostEstimate(flops=flops, bytes_accessed=moved, transcendentals=0)


def params(mib):
    return pltpu.CompilerParams(vmem_limit_bytes=mib << 20)


def block_of(device):
    z, half = device // 2, device % 2
    return jnp.where(half == 0, z, SEQ - 1 - z)


def peer(chunk):
    return chunk ^ (SEQ // 2)


def fold_source(position):
    period, phase = position // (2 * SEQ), position % (2 * SEQ)
    late = phase >= SEQ
    device = jnp.where(late, 2 * SEQ - 1 - phase, phase)
    return peer(device), 2 * period + late.astype(jnp.int32)


def pack_kernel(tokens, packed):
    shape = (packed.shape[0], tokens.shape[0])
    target, source = iota(shape, 0), iota(shape, 1)
    wanted = 4 * block_of(peer(target // 8)) + target % 4
    moved = None
    for part in range(2):
        pick = (source == wanted) & (target // 4 % 2 == part)
        term = dot(pick.astype(BF16), tokens[:, 128 * part : 128 * (part + 1)])
        moved = term if moved is None else moved + term
    packed[...] = moved.astype(BF16)


def unpack(packed, count):
    shape = (count, packed.shape[0])
    target, source = iota(shape, 0), iota(shape, 1)
    mine = block_of(peer(source // 8)) == target // 4
    halves = []
    for part in range(2):
        pick = mine & (source % 8 == 4 * part + target % 4)
        halves.append(dot(pick.astype(BF16), packed[...]).astype(BF16))
    return jnp.concatenate(halves, axis=1)


def unfold_kernel(received, spread):
    copies, rows, _ = spread.shape
    shape = (rows, received.shape[0])
    device, slot = fold_source(iota(shape, 0))
    column = iota(shape, 1)
    for part in range(2):
        pick = (column == device * 8 + part * 4 + slot).astype(BF16)
        moved = dot(pick, received[...]).astype(BF16)
        for copy in range(copies):
            spread[copy, :, 128 * part : 128 * (part + 1)] = moved


def refold(gated, outgoing):
    shape = (outgoing.shape[0], gated.shape[0])
    device, slot = fold_source(iota(shape, 1))
    target = iota(shape, 0)
    moved = None
    for part in range(2):
        pick = (target == device * 8 + part * 4 + slot).astype(BF16)
        term = dot(pick, gated[:, 128 * part : 128 * (part + 1)])
        moved = term if moved is None else moved + term
    outgoing[...] = moved.astype(BF16)


def sum_kernel(terms, mixed):
    total = terms[0].astype(F32)
    for term in range(1, terms.shape[0]):
        total = total + terms[term].astype(F32)
    mixed[...] = total.astype(BF16)


def segment_columns(segments, first, count):
    blocks = []
    for block in range(count):
        row = segments[pl.ds(first + block, 1), :].astype(F32)
        blocks.append(jnp.transpose(jnp.broadcast_to(row, (128, 128))))
    return jnp.concatenate(blocks, axis=0)


def short_conv(extended, columns, taps, lead):
    own = columns[lead:, :1]
    result = taps[0] * extended[lead:]
    for tap in range(1, taps.shape[0]):
        shifted = pltpu.roll(extended, tap, 0)[lead:]
        same = (pltpu.roll(columns, tap, 0)[lead:, :1] == own).astype(F32)
        result = result + taps[tap] * shifted * same
    return result


def join(blocks):
    return jnp.concatenate([blocks[chip] for chip in range(blocks.shape[0])], axis=1)


def project_near_kernel(rows, weights, partial, far_lines, lines, sems):
    core = lax.axis_index("chan") % 2
    chips, _, width = rows.shape
    copies = [
        pltpu.make_async_copy(weights.at[part, :, core], lines.at[part], sems.at[part])
        for part in range(3)
    ]
    copies.append(pltpu.make_async_copy(weights.at[:, :, 1 - core], far_lines, sems.at[3]))
    for copy in copies:
        copy.start()
    data = join(rows)
    for part in range(3):
        copies[part].wait()
        partial[part] = dot(data, lines[part].reshape(chips * width, width))
    copies[3].wait()


def project_far_kernel(rows, lines, partial, segments, short_filter, qkv, halo):
    chips, count, width = rows.shape
    data = join(rows)
    for part in range(3):
        total = partial[part] + dot(data, lines[part].reshape(chips * width, width))
        rounded = total.astype(BF16)
        qkv[part] = rounded
        halo[128 + 16 * part : 144 + 16 * part, :] = rounded[count - 16 :]
    block = block_of(lax.axis_index("seq"))
    columns = segment_columns(segments, 2 * block, 2)[count - 136 :]
    pair = []
    for part in (1, 2):
        extended = qkv[part].astype(F32)[count - 136 :]
        taps = jnp.stack([short_filter[tap, part : part + 1, :] for tap in range(3)])
        pair.append(short_conv(extended, columns, taps, 8))
    halo[:128, :] = (pair[0] * pair[1]).astype(BF16)


def band_kernel(filters, bands):
    groups, taps = filters.shape
    flip = iota((taps, 2 * taps), 1) == taps - iota((taps, 2 * taps), 0)
    first_rows = dot(filters[...], flip.astype(BF16))
    for group in range(groups):
        row = jnp.broadcast_to(first_rows[group : group + 1], (taps, 2 * taps))
        bands[group] = pltpu.roll(row, 0, 1, stride=1, stride_axis=0).astype(BF16)


def mix_kernel(qkv, halo, bands, segments, short_filter, skip_gain, outgoing, gated_out):
    seq = block_of(lax.axis_index("seq"))
    count, chans = gated_out.shape
    groups = bands.shape[0]
    size = chans // groups
    ahead = segment_columns(segments, jnp.maximum(2 * seq - 1, 0), 1)
    ahead = jnp.where(seq > 0, ahead, -1.0)
    columns = jnp.concatenate([ahead, segment_columns(segments, 2 * seq, 2)], axis=0)
    convolved = []
    for part in range(3):
        lead = halo[128 + 16 * part : 144 + 16 * part, :].astype(F32)[8:]
        extended = jnp.concatenate([lead, qkv[part].astype(F32)], axis=0)
        taps = jnp.stack([short_filter[tap, part : part + 1, :] for tap in range(3)])
        convolved.append(short_conv(extended, columns[120:], taps, 8))
    gated = (convolved[1] * convolved[2]).astype(BF16)
    gated_ext = jnp.concatenate([halo[:128, :], gated], axis=0)
    lane_group = iota((256, 128), 1) // size
    for block in range(count // 128):
        own = columns[128 * (block + 1) : 128 * (block + 2)]
        masks = [
            (own == jnp.transpose(columns[128 * (block + k) : 128 * (block + k + 1)]))
            for k in range(2)
        ]
        mask = jnp.concatenate(masks, axis=1).astype(F32).astype(BF16)
        for side in range(chans // 128):
            lanes = slice(128 * side, 128 * (side + 1))
            window = gated_ext[128 * block : 128 * block + 256, lanes]
            total = jnp.zeros((128, 128), F32)
            for group in range(128 // size):
                band = bands[side * (128 // size) + group] * mask
                chosen = jnp.where(lane_group == group, window, jnp.zeros((), BF16))
                total = total + dot(band, chosen)
            rows = slice(128 * block, 128 * (block + 1))
            direct = skip_gain[:, lanes] * gated[rows, lanes].astype(F32)
            gated_out[rows, lanes] = (convolved[0][rows, lanes] * (total + direct)).astype(BF16)
    refold(gated_out, outgoing)


def pick_kernel(weights, given, kept, sems):
    core = lax.axis_index("chan") % 2
    copies = []
    for i, (lines, parity) in enumerate(((given, 1 - core), (kept, core))):
        chips, _, width = lines.shape
        for chip in range(chips):
            columns = pl.ds(pl.multiple_of((2 * chip + parity) * width, width), width)
            copies.append(pltpu.make_async_copy(weights.at[:, columns], lines.at[chip], sems.at[i, chip]))
    for copy in copies:
        copy.start()
    for copy in copies:
        copy.wait()


def out_near_kernel(packed, lines, sums):
    rows = unpack(packed, sums.shape[1])
    for chip in range(sums.shape[0]):
        sums[chip] = dot(rows, lines[chip])


def out_far_kernel(packed, lines, near, sums):
    rows = unpack(packed, sums.shape[1])
    for chip in range(sums.shape[0]):
        sums[chip] = (near[chip] + dot(rows, lines[chip])).astype(BF16)


def kernel(body, name, out_shape, mib, flops, moved, in_place=(), scratch=()):
    vector = pl.BlockSpec(memory_space=pltpu.VMEM)
    anywhere = pl.BlockSpec(memory_space=pltpu.HBM)

    def call(*args):
        return pl.pallas_call(
            body,
            out_shape=out_shape,
            in_specs=[anywhere if i in in_place else vector for i in range(len(args))],
            out_specs=jax.tree.map(lambda _: vector, out_shape),
            scratch_shapes=scratch,
            compiler_params=params(mib),
            cost_estimate=cost(flops, moved),
            name=name,
        )(*args)

    return call


def array(shape, dtype=BF16):
    return jax.ShapeDtypeStruct(shape, dtype)


def over_seq(packed):
    chunks = packed.reshape(SEQ, 8, 128)
    order = [[peer(chunk) for chunk in range(SEQ)]]
    return lax.all_to_all(chunks, "seq", 0, 0, axis_index_groups=order, tiled=True).reshape(8 * SEQ, 128)


def body(tokens, w_in, short_filter, mr_filter, skip_gain, w_out, segments):
    rows, chans = tokens.shape
    width = w_in.shape[0]
    chan_count = lax.axis_size("chan")
    chips = chan_count // 2
    same_core = [[2 * chip + c for chip in range(chips)] for c in range(2)]
    partners = [(i, i ^ 1) for i in range(chan_count)]
    holder = {int(k): d for d, k in enumerate([d // 2 if d % 2 == 0 else SEQ - 1 - d // 2 for d in range(SEQ)])}
    ahead = [(holder[k], holder[k + 1]) for k in range(SEQ - 1)]
    segments = segments.reshape(-1, 128)
    gain = skip_gain.reshape(1, chans)
    moved = rows * chans * 2

    packed = kernel(pack_kernel, "pack", array((8 * SEQ, 128)), 4, 1 << 26, 2 * moved)(tokens)
    spread = kernel(unfold_kernel, "unfold", array((chips, rows, chans)), 8, 1 << 27, 9 * moved)(over_seq(packed))
    near = lax.all_to_all(spread, "chan", 0, 0, axis_index_groups=same_core, tiled=True)
    far = lax.ppermute(near, "chan", partners)
    bands = kernel(band_kernel, "bands", array((mr_filter.shape[0], 128, 256)), 8, 1 << 24, 8 * moved)(mr_filter)
    weights = w_in.transpose(1, 0, 2).reshape(3, chips, 2, chans, chans)
    lines = (3, chips, chans, chans)
    work = 3 * rows * width * chans
    partial, far_lines = kernel(
        project_near_kernel,
        "project_near",
        (array((3, rows, chans), F32), array(lines)),
        47,
        work,
        60 * moved,
        (1,),
        [pltpu.VMEM(lines, BF16), pltpu.SemaphoreType.DMA((4,))],
    )(near, weights)
    qkv, halo = kernel(
        project_far_kernel,
        "project_far",
        (array((3, rows, chans)), array((176, chans))),
        8,
        work,
        40 * moved,
    )(far, far_lines, partial, segments, short_filter)

    before = lax.ppermute(halo, "seq", ahead)
    block = array((chips, rows, chans))
    given, kept = kernel(
        pick_kernel, "pick", (block, block), 8, 0, 32 * moved, (0,), [pltpu.SemaphoreType.DMA((2, chips))]
    )(w_out)
    taken = lax.ppermute(given, "chan", partners)
    outgoing = kernel(
        mix_kernel, "mix", array((8 * SEQ, 128)), 8, 1 << 29, 16 * moved, (), [pltpu.VMEM((rows, chans), BF16)]
    )(qkv, before, bands, segments, short_filter, gain)
    returned = over_seq(outgoing)
    other = lax.ppermute(returned, "chan", partners)
    sums = kernel(out_near_kernel, "out_near", array(block.shape, F32), 8, work // 3, 16 * moved)(returned, kept)
    sums = kernel(out_far_kernel, "out_far", block, 8, work // 3, 16 * moved)(other, taken, sums)
    terms = lax.all_to_all(sums, "chan", 0, 0, axis_index_groups=same_core, tiled=True)
    return kernel(sum_kernel, "sum", array((rows, chans)), 4, 1 << 20, 9 * moved)(terms)


def solution(mesh):
    return jax.shard_map(
        body,
        mesh=mesh,
        in_specs=(
            P("seq", "chan"),
            P(None, None, "chan"),
            P(None, None, "chan"),
            P("chan", None),
            P("chan"),
            P("chan", None),
            P(),
        ),
        out_specs=P("seq", "chan"),
        check_vma=False,
    )
```

```python
import jax
import jax.numpy as jnp
from jax import lax
from jax.experimental import pallas as pl
from jax.experimental.pallas import tpu as pltpu
from jax.sharding import PartitionSpec as P

BF16 = jnp.bfloat16
F32 = jnp.float32
SEQ = 64
TURN_IN, TURN_OUT = 40, 34


def iota(shape, dim):
    return lax.broadcasted_iota(jnp.int32, shape, dim)


def dot(a, b):
    return jnp.dot(a, b, preferred_element_type=F32)


def cost(flops, moved):
    return pl.CostEstimate(flops=flops, bytes_accessed=moved, transcendentals=0)


def params(mib):
    return pltpu.CompilerParams(vmem_limit_bytes=mib << 20)


def block_of(device):
    z, half = device // 2, device % 2
    return jnp.where(half == 0, z, SEQ - 1 - z)


def device_at(chunk, turn):
    return (chunk + turn) & (SEQ - 1)


def fold_source(position, turn):
    period, phase = position // (2 * SEQ), position % (2 * SEQ)
    late = phase >= SEQ
    device = jnp.where(late, 2 * SEQ - 1 - phase, phase)
    return (device - turn) & (SEQ - 1), 2 * period + late.astype(jnp.int32)


def member(chip, core):
    return chip ^ (7 * core)


def pack_kernel(tokens, packed):
    shape = (packed.shape[0], tokens.shape[0])
    target, source = iota(shape, 0), iota(shape, 1)
    wanted = 4 * block_of(device_at(target // 8, TURN_IN)) + target % 4
    moved = None
    for part in range(2):
        pick = (source == wanted) & (target // 4 % 2 == part)
        term = dot(pick.astype(BF16), tokens[:, 128 * part : 128 * (part + 1)])
        moved = term if moved is None else moved + term
    packed[...] = moved.astype(BF16)


def unpack(packed, count):
    shape = (count, packed.shape[0])
    target, source = iota(shape, 0), iota(shape, 1)
    mine = block_of(device_at(source // 8, TURN_OUT)) == target // 4
    halves = []
    for part in range(2):
        pick = mine & (source % 8 == 4 * part + target % 4)
        halves.append(dot(pick.astype(BF16), packed[...]).astype(BF16))
    return jnp.concatenate(halves, axis=1)


def unfold_kernel(received, spread):
    copies, rows, _ = spread.shape
    shape = (rows, received.shape[0])
    device, slot = fold_source(iota(shape, 0), TURN_IN)
    column = iota(shape, 1)
    for part in range(2):
        pick = (column == device * 8 + part * 4 + slot).astype(BF16)
        moved = dot(pick, received[...]).astype(BF16)
        for copy in range(copies):
            spread[copy, :, 128 * part : 128 * (part + 1)] = moved


def refold(gated, outgoing):
    shape = (outgoing.shape[0], gated.shape[0])
    device, slot = fold_source(iota(shape, 1), TURN_OUT)
    target = iota(shape, 0)
    moved = None
    for part in range(2):
        pick = (target == device * 8 + part * 4 + slot).astype(BF16)
        term = dot(pick, gated[:, 128 * part : 128 * (part + 1)])
        moved = term if moved is None else moved + term
    outgoing[...] = moved.astype(BF16)


def sum_kernel(terms, mixed):
    total = terms[0].astype(F32)
    for term in range(1, terms.shape[0]):
        total = total + terms[term].astype(F32)
    mixed[...] = total.astype(BF16)


def segment_columns(segments, first, count):
    blocks = []
    for block in range(count):
        row = segments[pl.ds(first + block, 1), :].astype(F32)
        blocks.append(jnp.transpose(jnp.broadcast_to(row, (128, 128))))
    return jnp.concatenate(blocks, axis=0)


def short_conv(extended, columns, taps, lead):
    own = columns[lead:, :1]
    result = taps[0] * extended[lead:]
    for tap in range(1, taps.shape[0]):
        shifted = pltpu.roll(extended, tap, 0)[lead:]
        same = (pltpu.roll(columns, tap, 0)[lead:, :1] == own).astype(F32)
        result = result + taps[tap] * shifted * same
    return result


def join(blocks, core):
    return jnp.concatenate([blocks[member(chip, core)] for chip in range(blocks.shape[0])], axis=1)


def project_near_kernel(rows, weights, partial, far_lines, lines, sems):
    core = lax.axis_index("chan") % 2
    chips, _, width = rows.shape
    copies = [
        pltpu.make_async_copy(weights.at[part, :, core], lines.at[part], sems.at[part])
        for part in range(3)
    ]
    copies.append(pltpu.make_async_copy(weights.at[:, :, 1 - core], far_lines, sems.at[3]))
    for copy in copies:
        copy.start()
    data = join(rows, core)
    for part in range(3):
        copies[part].wait()
        partial[part] = dot(data, lines[part].reshape(chips * width, width))
    copies[3].wait()


def project_far_kernel(rows, lines, partial, segments, short_filter, qkv, halo):
    chips, count, width = rows.shape
    data = join(rows, 1 - lax.axis_index("chan") % 2)
    for part in range(3):
        total = partial[part] + dot(data, lines[part].reshape(chips * width, width))
        rounded = total.astype(BF16)
        qkv[part] = rounded
        halo[128 + 16 * part : 144 + 16 * part, :] = rounded[count - 16 :]
    block = block_of(lax.axis_index("seq"))
    columns = segment_columns(segments, 2 * block, 2)[count - 136 :]
    pair = []
    for part in (1, 2):
        extended = qkv[part].astype(F32)[count - 136 :]
        taps = jnp.stack([short_filter[tap, part : part + 1, :] for tap in range(3)])
        pair.append(short_conv(extended, columns, taps, 8))
    halo[:128, :] = (pair[0] * pair[1]).astype(BF16)


def band_kernel(filters, bands):
    groups, taps = filters.shape
    flip = iota((taps, 2 * taps), 1) == taps - iota((taps, 2 * taps), 0)
    first_rows = dot(filters[...], flip.astype(BF16))
    for group in range(groups):
        row = jnp.broadcast_to(first_rows[group : group + 1], (taps, 2 * taps))
        bands[group] = pltpu.roll(row, 0, 1, stride=1, stride_axis=0).astype(BF16)


def mix_kernel(qkv, halo, bands, segments, short_filter, skip_gain, outgoing, gated_out):
    seq = block_of(lax.axis_index("seq"))
    count, chans = gated_out.shape
    groups = bands.shape[0]
    size = chans // groups
    ahead = segment_columns(segments, jnp.maximum(2 * seq - 1, 0), 1)
    ahead = jnp.where(seq > 0, ahead, -1.0)
    columns = jnp.concatenate([ahead, segment_columns(segments, 2 * seq, 2)], axis=0)
    convolved = []
    for part in range(3):
        lead = halo[128 + 16 * part : 144 + 16 * part, :].astype(F32)[8:]
        extended = jnp.concatenate([lead, qkv[part].astype(F32)], axis=0)
        taps = jnp.stack([short_filter[tap, part : part + 1, :] for tap in range(3)])
        convolved.append(short_conv(extended, columns[120:], taps, 8))
    gated = (convolved[1] * convolved[2]).astype(BF16)
    gated_ext = jnp.concatenate([halo[:128, :], gated], axis=0)
    lane_group = iota((256, 128), 1) // size
    for block in range(count // 128):
        own = columns[128 * (block + 1) : 128 * (block + 2)]
        masks = [
            (own == jnp.transpose(columns[128 * (block + k) : 128 * (block + k + 1)]))
            for k in range(2)
        ]
        mask = jnp.concatenate(masks, axis=1).astype(F32).astype(BF16)
        for side in range(chans // 128):
            lanes = slice(128 * side, 128 * (side + 1))
            window = gated_ext[128 * block : 128 * block + 256, lanes]
            total = jnp.zeros((128, 128), F32)
            for group in range(128 // size):
                band = bands[side * (128 // size) + group] * mask
                chosen = jnp.where(lane_group == group, window, jnp.zeros((), BF16))
                total = total + dot(band, chosen)
            rows = slice(128 * block, 128 * (block + 1))
            direct = skip_gain[:, lanes] * gated[rows, lanes].astype(F32)
            gated_out[rows, lanes] = (convolved[0][rows, lanes] * (total + direct)).astype(BF16)
    refold(gated_out, outgoing)


def pick_kernel(weights, given, kept, sems):
    core = lax.axis_index("chan") % 2
    copies = []
    for i, (lines, parity) in enumerate(((given, 1 - core), (kept, core))):
        chips, _, width = lines.shape
        for chip in range(chips):
            columns = pl.ds(pl.multiple_of((2 * chip + parity) * width, width), width)
            copies.append(pltpu.make_async_copy(weights.at[:, columns], lines.at[chip], sems.at[i, chip]))
    for copy in copies:
        copy.start()
    for copy in copies:
        copy.wait()


def out_near_kernel(packed, lines, sums):
    rows = unpack(packed, sums.shape[1])
    core = lax.axis_index("chan") % 2
    for chip in range(sums.shape[0]):
        sums[member(chip, core)] = dot(rows, lines[chip])


def out_far_kernel(packed, lines, near, sums):
    rows = unpack(packed, sums.shape[1])
    core = lax.axis_index("chan") % 2
    for chip in range(sums.shape[0]):
        place = member(chip, core)
        sums[place] = (near[place] + dot(rows, lines[chip])).astype(BF16)


def kernel(body, name, out_shape, mib, flops, moved, in_place=(), scratch=()):
    vector = pl.BlockSpec(memory_space=pltpu.VMEM)
    anywhere = pl.BlockSpec(memory_space=pltpu.HBM)

    def call(*args):
        return pl.pallas_call(
            body,
            out_shape=out_shape,
            in_specs=[anywhere if i in in_place else vector for i in range(len(args))],
            out_specs=jax.tree.map(lambda _: vector, out_shape),
            scratch_shapes=scratch,
            compiler_params=params(mib),
            cost_estimate=cost(flops, moved),
            name=name,
        )(*args)

    return call


def array(shape, dtype=BF16):
    return jax.ShapeDtypeStruct(shape, dtype)


def over_seq(packed, turn):
    chunks = packed.reshape(SEQ, 8, 128)
    order = [[device_at(chunk, turn) for chunk in range(SEQ)]]
    return lax.all_to_all(chunks, "seq", 0, 0, axis_index_groups=order, tiled=True).reshape(8 * SEQ, 128)


def body(tokens, w_in, short_filter, mr_filter, skip_gain, w_out, segments):
    rows, chans = tokens.shape
    width = w_in.shape[0]
    chan_count = lax.axis_size("chan")
    chips = chan_count // 2
    same_core = [[2 * member(place, c) + c for place in range(chips)] for c in range(2)]
    partners = [(i, i ^ 1) for i in range(chan_count)]
    holder = {int(k): d for d, k in enumerate([d // 2 if d % 2 == 0 else SEQ - 1 - d // 2 for d in range(SEQ)])}
    ahead = [(holder[k], holder[k + 1]) for k in range(SEQ - 1)]
    segments = segments.reshape(-1, 128)
    gain = skip_gain.reshape(1, chans)
    moved = rows * chans * 2

    packed = kernel(pack_kernel, "pack", array((8 * SEQ, 128)), 4, 1 << 26, 2 * moved)(tokens)
    spread = kernel(unfold_kernel, "unfold", array((chips, rows, chans)), 8, 1 << 27, 9 * moved)(over_seq(packed, TURN_IN))
    near = lax.all_to_all(spread, "chan", 0, 0, axis_index_groups=same_core, tiled=True)
    far = lax.ppermute(near, "chan", partners)
    bands = kernel(band_kernel, "bands", array((mr_filter.shape[0], 128, 256)), 8, 1 << 24, 8 * moved)(mr_filter)
    weights = w_in.transpose(1, 0, 2).reshape(3, chips, 2, chans, chans)
    lines = (3, chips, chans, chans)
    work = 3 * rows * width * chans
    partial, far_lines = kernel(
        project_near_kernel,
        "project_near",
        (array((3, rows, chans), F32), array(lines)),
        47,
        work,
        60 * moved,
        (1,),
        [pltpu.VMEM(lines, BF16), pltpu.SemaphoreType.DMA((4,))],
    )(near, weights)
    qkv, halo = kernel(
        project_far_kernel,
        "project_far",
        (array((3, rows, chans)), array((176, chans))),
        8,
        work,
        40 * moved,
    )(far, far_lines, partial, segments, short_filter)

    before = lax.ppermute(halo, "seq", ahead)
    block = array((chips, rows, chans))
    given, kept = kernel(
        pick_kernel, "pick", (block, block), 8, 0, 32 * moved, (0,), [pltpu.SemaphoreType.DMA((2, chips))]
    )(w_out)
    taken = lax.ppermute(given, "chan", partners)
    outgoing = kernel(
        mix_kernel, "mix", array((8 * SEQ, 128)), 8, 1 << 29, 16 * moved, (), [pltpu.VMEM((rows, chans), BF16)]
    )(qkv, before, bands, segments, short_filter, gain)
    returned = over_seq(outgoing, TURN_OUT)
    other = lax.ppermute(returned, "chan", partners)
    sums = kernel(out_near_kernel, "out_near", array(block.shape, F32), 8, work // 3, 16 * moved)(returned, kept)
    sums = kernel(out_far_kernel, "out_far", block, 8, work // 3, 16 * moved)(other, taken, sums)
    terms = lax.all_to_all(sums, "chan", 0, 0, axis_index_groups=same_core, tiled=True)
    return kernel(sum_kernel, "sum", array((rows, chans)), 4, 1 << 20, 9 * moved)(terms)


def solution(mesh):
    return jax.shard_map(
        body,
        mesh=mesh,
        in_specs=(
            P("seq", "chan"),
            P(None, None, "chan"),
            P(None, None, "chan"),
            P("chan", None),
            P("chan"),
            P("chan", None),
            P(),
        ),
        out_specs=P("seq", "chan"),
        check_vma=False,
    )
```

```python
import jax
import jax.numpy as jnp
from jax import lax
from jax.experimental import pallas as pl
from jax.experimental.pallas import tpu as pltpu
from jax.sharding import PartitionSpec as P

BF16 = jnp.bfloat16
F32 = jnp.float32
SEQ = 64
TURN_IN, TURN_OUT = 40, 34


def iota(shape, dim):
    return lax.broadcasted_iota(jnp.int32, shape, dim)


def dot(a, b):
    return jnp.dot(a, b, preferred_element_type=F32)


def cost(flops, moved):
    return pl.CostEstimate(flops=flops, bytes_accessed=moved, transcendentals=0)


def params(mib):
    return pltpu.CompilerParams(vmem_limit_bytes=mib << 20)


def block_of(device):
    z, half = device // 2, device % 2
    return jnp.where(half == 0, z, SEQ - 1 - z)


def device_at(chunk, turn):
    return (chunk + turn) & (SEQ - 1)


def fold_source(position, turn):
    period, phase = position // (2 * SEQ), position % (2 * SEQ)
    late = phase >= SEQ
    device = jnp.where(late, 2 * SEQ - 1 - phase, phase)
    return (device - turn) & (SEQ - 1), 2 * period + late.astype(jnp.int32)


def member(chip, core):
    return chip ^ (7 * core)


def pack_kernel(tokens, packed):
    shape = (packed.shape[0], tokens.shape[0])
    target, source = iota((shape[0], 1), 0), iota(shape, 1)
    wanted = 4 * block_of(device_at(target // 8, TURN_IN)) + target % 4
    moved = None
    for part in range(2):
        pick = (source == wanted) & (target // 4 % 2 == part)
        term = dot(pick.astype(BF16), tokens[:, 128 * part : 128 * (part + 1)])
        moved = term if moved is None else moved + term
    packed[...] = moved.astype(BF16)


def unpack(packed, count):
    shape = (count, packed.shape[0])
    target, source = iota(shape, 0), iota((1, shape[1]), 1)
    mine = block_of(device_at(source // 8, TURN_OUT)) == target // 4
    halves = []
    for part in range(2):
        pick = mine & (source % 8 == 4 * part + target % 4)
        halves.append(dot(pick.astype(BF16), packed[...]).astype(BF16))
    return jnp.concatenate(halves, axis=1)


def unfold_kernel(received, spread):
    copies, rows, _ = spread.shape
    shape = (rows, received.shape[0])
    device, slot = fold_source(iota((shape[0], 1), 0), TURN_IN)
    column = iota(shape, 1)
    for part in range(2):
        pick = (column == device * 8 + part * 4 + slot).astype(BF16)
        moved = dot(pick, received[...]).astype(BF16)
        for copy in range(copies):
            spread[copy, :, 128 * part : 128 * (part + 1)] = moved


def refold_picks(picks):
    shape = picks.shape[1:]
    chunk, slot = fold_source(iota((1, shape[1]), 1), TURN_OUT)
    target = iota(shape, 0)
    for part in range(2):
        picks[part] = (target == chunk * 8 + part * 4 + slot).astype(BF16)


def sum_kernel(terms, mixed):
    total = terms[0].astype(F32)
    for term in range(1, terms.shape[0]):
        total = total + terms[term].astype(F32)
    mixed[...] = total.astype(BF16)


def segment_columns(segments, first, count):
    blocks = []
    for block in range(count):
        row = segments[pl.ds(first + block, 1), :].astype(F32)
        blocks.append(jnp.transpose(jnp.broadcast_to(row, (128, 128))))
    return jnp.concatenate(blocks, axis=0)


def short_conv(extended, columns, taps, lead):
    own = columns[lead:, :1]
    result = taps[0] * extended[lead:]
    for tap in range(1, taps.shape[0]):
        shifted = pltpu.roll(extended, tap, 0)[lead:]
        same = (pltpu.roll(columns, tap, 0)[lead:, :1] == own).astype(F32)
        result = result + taps[tap] * shifted * same
    return result


def join(blocks, core):
    return jnp.concatenate([blocks[member(chip, core)] for chip in range(blocks.shape[0])], axis=1)


def project_near_kernel(rows, weights, partial, far_lines, lines, sems):
    core = lax.axis_index("chan") % 2
    chips, _, width = rows.shape
    copies = [
        pltpu.make_async_copy(weights.at[part, :, core], lines.at[part], sems.at[part])
        for part in range(3)
    ]
    copies.append(pltpu.make_async_copy(weights.at[:, :, 1 - core], far_lines, sems.at[3]))
    for copy in copies:
        copy.start()
    data = join(rows, core)
    for part in range(3):
        copies[part].wait()
        partial[part] = dot(data, lines[part].reshape(chips * width, width))
    copies[3].wait()


def project_far_kernel(rows, lines, partial, segments, short_filter, qkv, halo):
    chips, count, width = rows.shape
    data = join(rows, 1 - lax.axis_index("chan") % 2)
    for part in range(3):
        total = partial[part] + dot(data, lines[part].reshape(chips * width, width))
        rounded = total.astype(BF16)
        qkv[part] = rounded
        halo[128 + 8 * part : 136 + 8 * part, :] = rounded[count - 8 :]
    block = block_of(lax.axis_index("seq"))
    columns = segment_columns(segments, 2 * block, 2)[count - 136 :]
    pair = []
    for part in (1, 2):
        extended = qkv[part].astype(F32)[count - 136 :]
        taps = jnp.stack([short_filter[tap, part : part + 1, :] for tap in range(3)])
        pair.append(short_conv(extended, columns, taps, 8))
    halo[:128, :] = (pair[0] * pair[1]).astype(BF16)


def band_kernel(filters, bands):
    groups, taps = filters.shape
    flip = iota((taps, 2 * taps), 1) == taps - iota((taps, 2 * taps), 0)
    first_rows = dot(filters[...], flip.astype(BF16))
    for group in range(groups):
        row = jnp.broadcast_to(first_rows[group : group + 1], (taps, 2 * taps))
        bands[group] = pltpu.roll(row, 0, 1, stride=1, stride_axis=0).astype(BF16)


def taps_of(short_filter, part):
    return jnp.stack([short_filter[tap, part : part + 1, :] for tap in range(short_filter.shape[0])])


def mask_of(columns, block):
    own = columns[128 * (block + 1) : 128 * (block + 2)]
    windows = [jnp.transpose(columns[128 * (block + k) : 128 * (block + k + 1)]) for k in range(2)]
    return jnp.concatenate([own == window for window in windows], axis=1).astype(F32).astype(BF16)


def extended_columns(segments, block):
    ahead = segment_columns(segments, jnp.maximum(2 * block - 1, 0), 1)
    ahead = jnp.where(block > 0, ahead, -1.0)
    return jnp.concatenate([ahead, segment_columns(segments, 2 * block, 2)], axis=0)


def banded(bands, window, side, rows, size):
    depth = window.shape[0]
    lane_group = iota(window.shape, 1) // size
    total = None
    for group in range(128 // size):
        chosen = jnp.where(lane_group == group, window, jnp.zeros((), BF16))
        term = dot(bands[side * (128 // size) + group, :rows, :depth], chosen)
        total = term if total is None else total + term
    return total


def mix_own_kernel(qkv, bands, segments, short_filter, skip_gain, queries, sums, masked, later, picks):
    _, count, chans = qkv.shape
    size = chans // bands.shape[0]
    columns = extended_columns(segments, block_of(lax.axis_index("seq")))
    convolved = []
    for part in range(3):
        extended = jnp.concatenate([jnp.zeros((8, chans), F32), qkv[part].astype(F32)], axis=0)
        convolved.append(short_conv(extended, columns[120:], taps_of(short_filter, part), 8))
    queries[...] = convolved[0]
    product = convolved[1] * convolved[2]
    gated = jnp.where(iota((count, 1), 0) >= 8, product, 0.0).astype(BF16)
    for block, target in enumerate((masked, later)):
        mask = mask_of(columns, block)
        for group in range(bands.shape[0]):
            target[group] = bands[group] * mask
    first = jnp.concatenate([jnp.zeros((128, chans), BF16), gated[:128]], axis=0)
    for side in range(chans // 128):
        lanes = slice(128 * side, 128 * (side + 1))
        for block, (source, window) in enumerate(((masked, first), (later, gated))):
            rows = slice(128 * block, 128 * (block + 1))
            direct = skip_gain[:, lanes] * gated[rows, lanes].astype(F32)
            sums[rows, lanes] = banded(source, window[:, lanes], side, 128, size) + direct
    refold_picks(picks)


def mix_rest_kernel(
    qkv, halo, masked, later, segments, short_filter, skip_gain, queries, sums, picks, outgoing, gated_out
):
    _, count, chans = qkv.shape
    size = chans // masked.shape[0]
    columns = extended_columns(segments, block_of(lax.axis_index("seq")))[120:136]
    convolved = []
    for part in range(3):
        lead = halo[128 + 8 * part : 136 + 8 * part, :].astype(F32)
        extended = jnp.concatenate([lead, qkv[part][:16].astype(F32)[:8]], axis=0)
        convolved.append(short_conv(extended, columns, taps_of(short_filter, part), 8))
    gated = (convolved[1] * convolved[2]).astype(BF16)
    window = jnp.concatenate([halo[:128, :], gated, jnp.zeros((120, chans), BF16)], axis=0)
    query = jnp.concatenate([convolved[0], queries[8:, :]], axis=0)
    for side in range(chans // 128):
        lanes = slice(128 * side, 128 * (side + 1))
        ahead = banded(masked, window[:, lanes], side, 128, size)
        across = banded(later, window[128:, lanes], side, 8, size)
        direct = skip_gain[:, lanes] * gated[:, lanes].astype(F32)
        total = sums[:, lanes] + jnp.concatenate([ahead, across, jnp.zeros((count - 136, 128), F32)], axis=0)
        total = jnp.concatenate([total[:8] + direct, total[8:]], axis=0)
        gated_out[:, lanes] = (query[:, lanes] * total).astype(BF16)
    moved = None
    for part in range(2):
        term = dot(picks[part], gated_out[:, 128 * part : 128 * (part + 1)])
        moved = term if moved is None else moved + term
    outgoing[...] = moved.astype(BF16)


def pick_kernel(weights, given, kept, sems):
    core = lax.axis_index("chan") % 2
    copies = []
    for i, (lines, parity) in enumerate(((given, 1 - core), (kept, core))):
        chips, _, width = lines.shape
        for chip in range(chips):
            columns = pl.ds(pl.multiple_of((2 * chip + parity) * width, width), width)
            copies.append(pltpu.make_async_copy(weights.at[:, columns], lines.at[chip], sems.at[i, chip]))
    for copy in copies:
        copy.start()
    for copy in copies:
        copy.wait()


def out_near_kernel(packed, lines, sums):
    rows = unpack(packed, sums.shape[1])
    core = lax.axis_index("chan") % 2
    for chip in range(sums.shape[0]):
        sums[member(chip, core)] = dot(rows, lines[chip])


def out_far_kernel(packed, lines, near, sums):
    rows = unpack(packed, sums.shape[1])
    core = lax.axis_index("chan") % 2
    for chip in range(sums.shape[0]):
        place = member(chip, core)
        sums[place] = (near[place] + dot(rows, lines[chip])).astype(BF16)


def kernel(body, name, out_shape, mib, flops, moved, in_place=(), scratch=()):
    vector = pl.BlockSpec(memory_space=pltpu.VMEM)
    anywhere = pl.BlockSpec(memory_space=pltpu.HBM)

    def call(*args):
        return pl.pallas_call(
            body,
            out_shape=out_shape,
            in_specs=[anywhere if i in in_place else vector for i in range(len(args))],
            out_specs=jax.tree.map(lambda _: vector, out_shape),
            scratch_shapes=scratch,
            compiler_params=params(mib),
            cost_estimate=cost(flops, moved),
            name=name,
        )(*args)

    return call


def array(shape, dtype=BF16):
    return jax.ShapeDtypeStruct(shape, dtype)


def over_seq(packed, turn):
    chunks = packed.reshape(SEQ, 8, 128)
    order = [[device_at(chunk, turn) for chunk in range(SEQ)]]
    return lax.all_to_all(chunks, "seq", 0, 0, axis_index_groups=order, tiled=True).reshape(8 * SEQ, 128)


def body(tokens, w_in, short_filter, mr_filter, skip_gain, w_out, segments):
    rows, chans = tokens.shape
    width = w_in.shape[0]
    chan_count = lax.axis_size("chan")
    chips = chan_count // 2
    same_core = [[2 * member(place, c) + c for place in range(chips)] for c in range(2)]
    partners = [(i, i ^ 1) for i in range(chan_count)]
    holder = {int(k): d for d, k in enumerate([d // 2 if d % 2 == 0 else SEQ - 1 - d // 2 for d in range(SEQ)])}
    ahead = [(holder[k], holder[k + 1]) for k in range(SEQ - 1)]
    segments = segments.reshape(-1, 128)
    gain = skip_gain.reshape(1, chans)
    moved = rows * chans * 2

    packed = kernel(pack_kernel, "pack", array((8 * SEQ, 128)), 4, 1 << 26, 2 * moved)(tokens)
    spread = kernel(unfold_kernel, "unfold", array((chips, rows, chans)), 8, 1 << 27, 9 * moved)(over_seq(packed, TURN_IN))
    near = lax.all_to_all(spread, "chan", 0, 0, axis_index_groups=same_core, tiled=True)
    far = lax.ppermute(near, "chan", partners)
    bands = kernel(band_kernel, "bands", array((mr_filter.shape[0], 128, 256)), 8, 1 << 24, 8 * moved)(mr_filter)
    weights = w_in.transpose(1, 0, 2).reshape(3, chips, 2, chans, chans)
    lines = (3, chips, chans, chans)
    work = 3 * rows * width * chans
    partial, far_lines = kernel(
        project_near_kernel,
        "project_near",
        (array((3, rows, chans), F32), array(lines)),
        47,
        work,
        60 * moved,
        (1,),
        [pltpu.VMEM(lines, BF16), pltpu.SemaphoreType.DMA((4,))],
    )(near, weights)
    qkv, halo = kernel(
        project_far_kernel,
        "project_far",
        (array((3, rows, chans)), array((152, chans))),
        8,
        work,
        40 * moved,
    )(far, far_lines, partial, segments, short_filter)

    before = lax.ppermute(halo, "seq", ahead)
    block = array((chips, rows, chans))
    given, kept = kernel(
        pick_kernel, "pick", (block, block), 8, 0, 32 * moved, (0,), [pltpu.SemaphoreType.DMA((2, chips))]
    )(w_out)
    taken = lax.ppermute(given, "chan", partners)
    wide = array((rows, chans), F32)
    queries, own, masked, later, picks = kernel(
        mix_own_kernel,
        "mix_own",
        (wide, wide, array(bands.shape), array(bands.shape), array((2, 8 * SEQ, rows))),
        8,
        1 << 29,
        32 * moved,
    )(qkv, bands, segments, short_filter, gain)
    outgoing = kernel(
        mix_rest_kernel, "mix_rest", array((8 * SEQ, 128)), 8, 1 << 28, 32 * moved, (), [pltpu.VMEM((rows, chans), BF16)]
    )(qkv, before, masked, later, segments, short_filter, gain, queries, own, picks)
    returned = over_seq(outgoing, TURN_OUT)
    other = lax.ppermute(returned, "chan", partners)
    sums = kernel(out_near_kernel, "out_near", array(block.shape, F32), 8, work // 3, 16 * moved)(returned, kept)
    sums = kernel(out_far_kernel, "out_far", block, 8, work // 3, 16 * moved)(other, taken, sums)
    terms = lax.all_to_all(sums, "chan", 0, 0, axis_index_groups=same_core, tiled=True)
    return kernel(sum_kernel, "sum", array((rows, chans)), 4, 1 << 20, 9 * moved)(terms)


def solution(mesh):
    return jax.shard_map(
        body,
        mesh=mesh,
        in_specs=(
            P("seq", "chan"),
            P(None, None, "chan"),
            P(None, None, "chan"),
            P("chan", None),
            P("chan"),
            P("chan", None),
            P(),
        ),
        out_specs=P("seq", "chan"),
        check_vma=False,
    )
```

```python
import jax
import jax.numpy as jnp
from jax import lax
from jax.experimental import pallas as pl
from jax.experimental.pallas import tpu as pltpu
from jax.sharding import PartitionSpec as P

BF16 = jnp.bfloat16
F32 = jnp.float32
SEQ = 64
TURN_IN, TURN_OUT = 40, 34


def iota(shape, dim):
    return lax.broadcasted_iota(jnp.int32, shape, dim)


def dot(a, b):
    return jnp.dot(a, b, preferred_element_type=F32)


def cost(flops, moved):
    return pl.CostEstimate(flops=flops, bytes_accessed=moved, transcendentals=0)


def params(mib):
    return pltpu.CompilerParams(vmem_limit_bytes=mib << 20)


def block_of(device):
    z, half = device // 2, device % 2
    return jnp.where(half == 0, z, SEQ - 1 - z)


def device_at(chunk, turn):
    return (chunk + turn) & (SEQ - 1)


def fold_source(position, turn):
    period, phase = position // (2 * SEQ), position % (2 * SEQ)
    late = phase >= SEQ
    device = jnp.where(late, 2 * SEQ - 1 - phase, phase)
    return (device - turn) & (SEQ - 1), 2 * period + late.astype(jnp.int32)


def member(chip, core):
    return chip ^ (7 * core)


def pack_kernel(tokens, packed):
    shape = (packed.shape[0], tokens.shape[0])
    target, source = iota((shape[0], 1), 0), iota(shape, 1)
    wanted = 4 * block_of(device_at(target // 8, TURN_IN)) + target % 4
    moved = None
    for part in range(2):
        pick = (source == wanted) & (target // 4 % 2 == part)
        term = dot(pick.astype(BF16), tokens[:, 128 * part : 128 * (part + 1)])
        moved = term if moved is None else moved + term
    packed[...] = moved.astype(BF16)


def unpack(packed, count):
    shape = (count, packed.shape[0])
    target, source = iota(shape, 0), iota((1, shape[1]), 1)
    mine = block_of(device_at(source // 8, TURN_OUT)) == target // 4
    halves = []
    for part in range(2):
        pick = mine & (source % 8 == 4 * part + target % 4)
        halves.append(dot(pick.astype(BF16), packed[...]).astype(BF16))
    return jnp.concatenate(halves, axis=1)


def unfold_kernel(received, spread):
    copies, rows, _ = spread.shape
    shape = (rows, received.shape[0])
    device, slot = fold_source(iota((shape[0], 1), 0), TURN_IN)
    column = iota(shape, 1)
    for part in range(2):
        pick = (column == device * 8 + part * 4 + slot).astype(BF16)
        moved = dot(pick, received[...]).astype(BF16)
        for copy in range(copies):
            spread[copy, :, 128 * part : 128 * (part + 1)] = moved


def refold_picks(picks):
    shape = picks.shape[1:]
    chunk, slot = fold_source(iota((1, shape[1]), 1), TURN_OUT)
    target = iota(shape, 0)
    for part in range(2):
        picks[part] = (target == chunk * 8 + part * 4 + slot).astype(BF16)


def sum_kernel(terms, mixed):
    total = terms[0].astype(F32)
    for term in range(1, terms.shape[0]):
        total = total + terms[term].astype(F32)
    mixed[...] = total.astype(BF16)


def segment_columns(segments, first, count):
    blocks = []
    for block in range(count):
        row = segments[pl.ds(first + block, 1), :].astype(F32)
        blocks.append(jnp.transpose(jnp.broadcast_to(row, (128, 128))))
    return jnp.concatenate(blocks, axis=0)


def short_conv(extended, columns, taps, lead):
    own = columns[lead:, :1]
    result = taps[0] * extended[lead:]
    for tap in range(1, taps.shape[0]):
        shifted = pltpu.roll(extended, tap, 0)[lead:]
        same = (pltpu.roll(columns, tap, 0)[lead:, :1] == own).astype(F32)
        result = result + taps[tap] * shifted * same
    return result


def join(blocks, core):
    return jnp.concatenate([blocks[member(chip, core)] for chip in range(blocks.shape[0])], axis=1)


def project_near_kernel(rows, weights, partial, far_lines, lines, sems):
    core = lax.axis_index("chan") % 2
    chips, _, width = rows.shape
    copies = [
        pltpu.make_async_copy(weights.at[part, :, core], lines.at[part], sems.at[part])
        for part in range(3)
    ]
    copies.append(pltpu.make_async_copy(weights.at[:, :, 1 - core], far_lines, sems.at[3]))
    for copy in copies:
        copy.start()
    data = join(rows, core)
    for part in range(3):
        copies[part].wait()
        partial[part] = dot(data, lines[part].reshape(chips * width, width))
    copies[3].wait()


def project_far_kernel(rows, lines, partial, segments, short_filter, qkv, halo):
    chips, count, width = rows.shape
    data = join(rows, 1 - lax.axis_index("chan") % 2)
    for part in range(3):
        total = partial[part] + dot(data, lines[part].reshape(chips * width, width))
        rounded = total.astype(BF16)
        qkv[part] = rounded
        halo[128 + 8 * part : 136 + 8 * part, :] = rounded[count - 8 :]
    block = block_of(lax.axis_index("seq"))
    columns = segment_columns(segments, 2 * block, 2)[count - 136 :]
    pair = []
    for part in (1, 2):
        extended = qkv[part].astype(F32)[count - 136 :]
        taps = jnp.stack([short_filter[tap, part : part + 1, :] for tap in range(3)])
        pair.append(short_conv(extended, columns, taps, 8))
    halo[:128, :] = (pair[0] * pair[1]).astype(BF16)


def band_kernel(filters, bands):
    groups, taps = filters.shape
    flip = iota((taps, 2 * taps), 1) == taps - iota((taps, 2 * taps), 0)
    first_rows = dot(filters[...], flip.astype(BF16))
    for group in range(groups):
        row = jnp.broadcast_to(first_rows[group : group + 1], (taps, 2 * taps))
        bands[group] = pltpu.roll(row, 0, 1, stride=1, stride_axis=0).astype(BF16)


def taps_of(short_filter, part):
    return jnp.stack([short_filter[tap, part : part + 1, :] for tap in range(short_filter.shape[0])])


def mask_of(columns, block):
    own = columns[128 * (block + 1) : 128 * (block + 2)]
    windows = [jnp.transpose(columns[128 * (block + k) : 128 * (block + k + 1)]) for k in range(2)]
    return jnp.concatenate([own == window for window in windows], axis=1).astype(F32).astype(BF16)


def extended_columns(segments, block):
    ahead = segment_columns(segments, jnp.maximum(2 * block - 1, 0), 1)
    ahead = jnp.where(block > 0, ahead, -1.0)
    return jnp.concatenate([ahead, segment_columns(segments, 2 * block, 2)], axis=0)


def banded(bands, window, side, size):
    lane_group = iota(window.shape, 1) // size
    total = None
    for group in range(128 // size):
        chosen = jnp.where(lane_group == group, window, jnp.zeros((), BF16))
        term = dot(bands[side * (128 // size) + group], chosen)
        total = term if total is None else total + term
    return total


def mix_own_kernel(
    qkv, bands, segments, short_filter, skip_gain, queries, sums, first, edge, picks, masked
):
    _, count, chans = qkv.shape
    groups = bands.shape[0]
    size = chans // groups
    columns = extended_columns(segments, block_of(lax.axis_index("seq")))
    edge[...] = columns[120:136]
    convolved = []
    for part in range(3):
        extended = jnp.concatenate([jnp.zeros((8, chans), F32), qkv[part].astype(F32)], axis=0)
        convolved.append(short_conv(extended, columns[120:], taps_of(short_filter, part), 8))
    queries[...] = convolved[0]
    product = convolved[1] * convolved[2]
    gated = jnp.where(iota((count, 1), 0) >= 8, product, 0.0).astype(BF16)
    mask = mask_of(columns, 0)
    for group in range(groups):
        first[group, :128] = bands[group] * mask
    mask = mask_of(columns, 1)
    for group in range(groups):
        later = bands[group] * mask
        masked[group] = later
        first[group, 128:] = jnp.concatenate([jnp.zeros((8, 128), BF16), later[:8, :128]], axis=1)
    ahead = jnp.concatenate([jnp.zeros((128, chans), BF16), gated[:128]], axis=0)
    for side in range(chans // 128):
        lanes = slice(128 * side, 128 * (side + 1))
        for block, window in enumerate((ahead, gated)):
            rows = slice(128 * block, 128 * (block + 1))
            direct = skip_gain[:, lanes] * gated[rows, lanes].astype(F32)
            source = first.at[:, :128] if block == 0 else masked
            sums[rows, lanes] = banded(source, window[:, lanes], side, size) + direct
    refold_picks(picks)


def mix_rest_kernel(
    qkv, halo, first, edge, short_filter, skip_gain, queries, sums, picks, outgoing, gated_out
):
    _, count, chans = qkv.shape
    size = chans // first.shape[0]
    convolved = []
    for part in range(3):
        lead = halo[128 + 8 * part : 136 + 8 * part, :].astype(F32)
        extended = jnp.concatenate([lead, qkv[part][:16].astype(F32)[:8]], axis=0)
        convolved.append(short_conv(extended, edge[...], taps_of(short_filter, part), 8))
    gated = (convolved[1] * convolved[2]).astype(BF16)
    window = jnp.concatenate([halo[:128, :], gated, jnp.zeros((120, chans), BF16)], axis=0)
    query = jnp.concatenate([convolved[0], queries[8:, :]], axis=0)
    for side in range(chans // 128):
        lanes = slice(128 * side, 128 * (side + 1))
        added = banded(first, window[:, lanes], side, size)
        direct = skip_gain[:, lanes] * gated[:, lanes].astype(F32)
        added = jnp.concatenate(
            [added[:8] + direct, added[8:], jnp.zeros((count - 136, 128), F32)], axis=0
        )
        gated_out[:, lanes] = (query[:, lanes] * (sums[:, lanes] + added)).astype(BF16)
    moved = None
    for part in range(2):
        term = dot(picks[part], gated_out[:, 128 * part : 128 * (part + 1)])
        moved = term if moved is None else moved + term
    outgoing[...] = moved.astype(BF16)


def pick_kernel(weights, given, kept, sems):
    core = lax.axis_index("chan") % 2
    copies = []
    for i, (lines, parity) in enumerate(((given, 1 - core), (kept, core))):
        chips, _, width = lines.shape
        for chip in range(chips):
            columns = pl.ds(pl.multiple_of((2 * chip + parity) * width, width), width)
            copies.append(pltpu.make_async_copy(weights.at[:, columns], lines.at[chip], sems.at[i, chip]))
    for copy in copies:
        copy.start()
    for copy in copies:
        copy.wait()


def out_near_kernel(packed, lines, sums):
    rows = unpack(packed, sums.shape[1])
    core = lax.axis_index("chan") % 2
    for chip in range(sums.shape[0]):
        sums[member(chip, core)] = dot(rows, lines[chip])


def out_far_kernel(packed, lines, near, sums):
    rows = unpack(packed, sums.shape[1])
    core = lax.axis_index("chan") % 2
    for chip in range(sums.shape[0]):
        place = member(chip, core)
        sums[place] = (near[place] + dot(rows, lines[chip])).astype(BF16)


def kernel(body, name, out_shape, mib, flops, moved, in_place=(), scratch=()):
    vector = pl.BlockSpec(memory_space=pltpu.VMEM)
    anywhere = pl.BlockSpec(memory_space=pltpu.HBM)

    def call(*args):
        return pl.pallas_call(
            body,
            out_shape=out_shape,
            in_specs=[anywhere if i in in_place else vector for i in range(len(args))],
            out_specs=jax.tree.map(lambda _: vector, out_shape),
            scratch_shapes=scratch,
            compiler_params=params(mib),
            cost_estimate=cost(flops, moved),
            name=name,
        )(*args)

    return call


def array(shape, dtype=BF16):
    return jax.ShapeDtypeStruct(shape, dtype)


def over_seq(packed, turn):
    chunks = packed.reshape(SEQ, 8, 128)
    order = [[device_at(chunk, turn) for chunk in range(SEQ)]]
    return lax.all_to_all(chunks, "seq", 0, 0, axis_index_groups=order, tiled=True).reshape(8 * SEQ, 128)


def body(tokens, w_in, short_filter, mr_filter, skip_gain, w_out, segments):
    rows, chans = tokens.shape
    width = w_in.shape[0]
    chan_count = lax.axis_size("chan")
    chips = chan_count // 2
    same_core = [[2 * member(place, c) + c for place in range(chips)] for c in range(2)]
    partners = [(i, i ^ 1) for i in range(chan_count)]
    holder = {int(k): d for d, k in enumerate([d // 2 if d % 2 == 0 else SEQ - 1 - d // 2 for d in range(SEQ)])}
    ahead = [(holder[k], holder[k + 1]) for k in range(SEQ - 1)]
    segments = segments.reshape(-1, 128)
    gain = skip_gain.reshape(1, chans)
    moved = rows * chans * 2

    packed = kernel(pack_kernel, "pack", array((8 * SEQ, 128)), 4, 1 << 26, 2 * moved)(tokens)
    spread = kernel(unfold_kernel, "unfold", array((chips, rows, chans)), 8, 1 << 27, 9 * moved)(over_seq(packed, TURN_IN))
    near = lax.all_to_all(spread, "chan", 0, 0, axis_index_groups=same_core, tiled=True)
    far = lax.ppermute(near, "chan", partners)
    bands = kernel(band_kernel, "bands", array((mr_filter.shape[0], 128, 256)), 8, 1 << 24, 8 * moved)(mr_filter)
    weights = w_in.transpose(1, 0, 2).reshape(3, chips, 2, chans, chans)
    lines = (3, chips, chans, chans)
    work = 3 * rows * width * chans
    partial, far_lines = kernel(
        project_near_kernel,
        "project_near",
        (array((3, rows, chans), F32), array(lines)),
        47,
        work,
        60 * moved,
        (1,),
        [pltpu.VMEM(lines, BF16), pltpu.SemaphoreType.DMA((4,))],
    )(near, weights)
    qkv, halo = kernel(
        project_far_kernel,
        "project_far",
        (array((3, rows, chans)), array((152, chans))),
        8,
        work,
        40 * moved,
    )(far, far_lines, partial, segments, short_filter)

    before = lax.ppermute(halo, "seq", ahead)
    block = array((chips, rows, chans))
    given, kept = kernel(
        pick_kernel, "pick", (block, block), 8, 0, 32 * moved, (0,), [pltpu.SemaphoreType.DMA((2, chips))]
    )(w_out)
    taken = lax.ppermute(given, "chan", partners)
    wide = array((rows, chans), F32)
    groups = mr_filter.shape[0]
    queries, own, first, edge, picks = kernel(
        mix_own_kernel,
        "mix_own",
        (wide, wide, array((groups, 136, 256)), array((16, 128), F32), array((2, 8 * SEQ, rows))),
        8,
        1 << 29,
        32 * moved,
        (),
        [pltpu.VMEM(bands.shape, BF16)],
    )(qkv, bands, segments, short_filter, gain)
    outgoing = kernel(
        mix_rest_kernel, "mix_rest", array((8 * SEQ, 128)), 8, 1 << 28, 32 * moved, (), [pltpu.VMEM((rows, chans), BF16)]
    )(qkv, before, first, edge, short_filter, gain, queries, own, picks)
    returned = over_seq(outgoing, TURN_OUT)
    other = lax.ppermute(returned, "chan", partners)
    sums = kernel(out_near_kernel, "out_near", array(block.shape, F32), 8, work // 3, 16 * moved)(returned, kept)
    sums = kernel(out_far_kernel, "out_far", block, 8, work // 3, 16 * moved)(other, taken, sums)
    terms = lax.all_to_all(sums, "chan", 0, 0, axis_index_groups=same_core, tiled=True)
    return kernel(sum_kernel, "sum", array((rows, chans)), 4, 1 << 20, 9 * moved)(terms)


def solution(mesh):
    return jax.shard_map(
        body,
        mesh=mesh,
        in_specs=(
            P("seq", "chan"),
            P(None, None, "chan"),
            P(None, None, "chan"),
            P("chan", None),
            P("chan"),
            P("chan", None),
            P(),
        ),
        out_specs=P("seq", "chan"),
        check_vma=False,
    )
```

```python
import jax
import jax.numpy as jnp
from jax import lax
from jax.experimental import pallas as pl
from jax.experimental.pallas import tpu as pltpu
from jax.sharding import PartitionSpec as P

BF16 = jnp.bfloat16
F32 = jnp.float32
SEQ = 64
TURN_IN, TURN_OUT = 36, 34


def iota(shape, dim):
    return lax.broadcasted_iota(jnp.int32, shape, dim)


def dot(a, b):
    return jnp.dot(a, b, preferred_element_type=F32)


def cost(flops, moved):
    return pl.CostEstimate(flops=flops, bytes_accessed=moved, transcendentals=0)


def params(mib):
    return pltpu.CompilerParams(vmem_limit_bytes=mib << 20)


def block_of(device):
    z, half = device // 2, device % 2
    return jnp.where(half == 0, z, SEQ - 1 - z)


def device_at(chunk, turn):
    return (chunk + turn) & (SEQ - 1)


def fold_source(position, turn):
    period, phase = position // (2 * SEQ), position % (2 * SEQ)
    late = phase >= SEQ
    device = jnp.where(late, 2 * SEQ - 1 - phase, phase)
    return (device - turn) & (SEQ - 1), 2 * period + late.astype(jnp.int32)


def member(chip, core):
    return chip ^ (7 * core)


def pack_kernel(tokens, packed):
    shape = (packed.shape[0], tokens.shape[0])
    target, source = iota((shape[0], 1), 0), iota(shape, 1)
    wanted = 4 * block_of(device_at(target // 8, TURN_IN)) + target % 4
    moved = None
    for part in range(2):
        pick = (source == wanted) & (target // 4 % 2 == part)
        term = dot(pick.astype(BF16), tokens[:, 128 * part : 128 * (part + 1)])
        moved = term if moved is None else moved + term
    packed[...] = moved.astype(BF16)


def unpack(packed, count):
    shape = (count, packed.shape[0])
    target, source = iota(shape, 0), iota((1, shape[1]), 1)
    mine = block_of(device_at(source // 8, TURN_OUT)) == target // 4
    halves = []
    for part in range(2):
        pick = mine & (source % 8 == 4 * part + target % 4)
        halves.append(dot(pick.astype(BF16), packed[...]).astype(BF16))
    return jnp.concatenate(halves, axis=1)


def unfold_kernel(received, spread):
    copies, rows, _ = spread.shape
    shape = (rows, received.shape[0])
    device, slot = fold_source(iota((shape[0], 1), 0), TURN_IN)
    column = iota(shape, 1)
    for part in range(2):
        pick = (column == device * 8 + part * 4 + slot).astype(BF16)
        moved = dot(pick, received[...]).astype(BF16)
        for copy in range(copies):
            spread[copy, :, 128 * part : 128 * (part + 1)] = moved


def refold_picks(picks):
    shape = picks.shape[1:]
    chunk, slot = fold_source(iota((1, shape[1]), 1), TURN_OUT)
    target = iota(shape, 0)
    for part in range(2):
        picks[part] = (target == chunk * 8 + part * 4 + slot).astype(BF16)


def sum_kernel(terms, mixed):
    total = terms[0].astype(F32)
    for term in range(1, terms.shape[0]):
        total = total + terms[term].astype(F32)
    mixed[...] = total.astype(BF16)


def segment_columns(segments, first, count):
    blocks = []
    for block in range(count):
        row = segments[pl.ds(first + block, 1), :].astype(F32)
        blocks.append(jnp.transpose(jnp.broadcast_to(row, (128, 128))))
    return jnp.concatenate(blocks, axis=0)


def short_conv(extended, columns, taps, lead):
    own = columns[lead:, :1]
    result = taps[0] * extended[lead:]
    for tap in range(1, taps.shape[0]):
        shifted = pltpu.roll(extended, tap, 0)[lead:]
        same = (pltpu.roll(columns, tap, 0)[lead:, :1] == own).astype(F32)
        result = result + taps[tap] * shifted * same
    return result


def join(blocks, core):
    return jnp.concatenate([blocks[member(chip, core)] for chip in range(blocks.shape[0])], axis=1)


def project_near_kernel(rows, weights, partial, far_lines, lines, sems):
    core = lax.axis_index("chan") % 2
    chips, _, width = rows.shape
    copies = [
        pltpu.make_async_copy(weights.at[part, :, core], lines.at[part], sems.at[part])
        for part in range(3)
    ]
    copies.append(pltpu.make_async_copy(weights.at[:, :, 1 - core], far_lines, sems.at[3]))
    for copy in copies:
        copy.start()
    data = join(rows, core)
    for part in range(3):
        copies[part].wait()
        partial[part] = dot(data, lines[part].reshape(chips * width, width))
    copies[3].wait()


def project_far_kernel(rows, lines, partial, segments, short_filter, qkv, halo):
    chips, count, width = rows.shape
    data = join(rows, 1 - lax.axis_index("chan") % 2)
    for part in range(3):
        total = partial[part] + dot(data, lines[part].reshape(chips * width, width))
        rounded = total.astype(BF16)
        qkv[part] = rounded
        halo[128 + 8 * part : 136 + 8 * part, :] = rounded[count - 8 :]
    block = block_of(lax.axis_index("seq"))
    columns = segment_columns(segments, 2 * block, 2)[count - 136 :]
    pair = []
    for part in (1, 2):
        extended = qkv[part].astype(F32)[count - 136 :]
        taps = jnp.stack([short_filter[tap, part : part + 1, :] for tap in range(3)])
        pair.append(short_conv(extended, columns, taps, 8))
    halo[:128, :] = (pair[0] * pair[1]).astype(BF16)


def band_kernel(filters, bands):
    groups, taps = filters.shape
    flip = iota((taps, 2 * taps), 1) == taps - iota((taps, 2 * taps), 0)
    first_rows = dot(filters[...], flip.astype(BF16))
    for group in range(groups):
        row = jnp.broadcast_to(first_rows[group : group + 1], (taps, 2 * taps))
        bands[group] = pltpu.roll(row, 0, 1, stride=1, stride_axis=0).astype(BF16)


def taps_of(short_filter, part):
    return jnp.stack([short_filter[tap, part : part + 1, :] for tap in range(short_filter.shape[0])])


def mask_of(columns, block):
    own = columns[128 * (block + 1) : 128 * (block + 2)]
    windows = [jnp.transpose(columns[128 * (block + k) : 128 * (block + k + 1)]) for k in range(2)]
    return jnp.concatenate([own == window for window in windows], axis=1).astype(F32).astype(BF16)


def extended_columns(segments, block):
    ahead = segment_columns(segments, jnp.maximum(2 * block - 1, 0), 1)
    ahead = jnp.where(block > 0, ahead, -1.0)
    return jnp.concatenate([ahead, segment_columns(segments, 2 * block, 2)], axis=0)


def banded(bands, window, side, size):
    lane_group = iota(window.shape, 1) // size
    total = None
    for group in range(128 // size):
        chosen = jnp.where(lane_group == group, window, jnp.zeros((), BF16))
        term = dot(bands[side * (128 // size) + group], chosen)
        total = term if total is None else total + term
    return total


def mix_own_kernel(
    qkv, bands, segments, short_filter, skip_gain, queries, sums, first, edge, picks, masked
):
    _, count, chans = qkv.shape
    groups = bands.shape[0]
    size = chans // groups
    columns = extended_columns(segments, block_of(lax.axis_index("seq")))
    edge[...] = columns[120:136]
    convolved = []
    for part in range(3):
        extended = jnp.concatenate([jnp.zeros((8, chans), F32), qkv[part].astype(F32)], axis=0)
        convolved.append(short_conv(extended, columns[120:], taps_of(short_filter, part), 8))
    queries[...] = convolved[0]
    product = convolved[1] * convolved[2]
    gated = jnp.where(iota((count, 1), 0) >= 8, product, 0.0).astype(BF16)
    mask = mask_of(columns, 0)
    for group in range(groups):
        first[group, :128] = bands[group] * mask
    mask = mask_of(columns, 1)
    for group in range(groups):
        later = bands[group] * mask
        masked[group] = later
        first[group, 128:] = jnp.concatenate([jnp.zeros((8, 128), BF16), later[:8, :128]], axis=1)
    ahead = jnp.concatenate([jnp.zeros((128, chans), BF16), gated[:128]], axis=0)
    for side in range(chans // 128):
        lanes = slice(128 * side, 128 * (side + 1))
        for block, window in enumerate((ahead, gated)):
            rows = slice(128 * block, 128 * (block + 1))
            direct = skip_gain[:, lanes] * gated[rows, lanes].astype(F32)
            source = first.at[:, :128] if block == 0 else masked
            sums[rows, lanes] = banded(source, window[:, lanes], side, size) + direct
    refold_picks(picks)


def mix_rest_kernel(
    qkv, halo, first, edge, short_filter, skip_gain, queries, sums, picks, outgoing, gated_out
):
    _, count, chans = qkv.shape
    size = chans // first.shape[0]
    convolved = []
    for part in range(3):
        lead = halo[128 + 8 * part : 136 + 8 * part, :].astype(F32)
        extended = jnp.concatenate([lead, qkv[part][:16].astype(F32)[:8]], axis=0)
        convolved.append(short_conv(extended, edge[...], taps_of(short_filter, part), 8))
    gated = (convolved[1] * convolved[2]).astype(BF16)
    window = jnp.concatenate([halo[:128, :], gated, jnp.zeros((120, chans), BF16)], axis=0)
    query = jnp.concatenate([convolved[0], queries[8:, :]], axis=0)
    for side in range(chans // 128):
        lanes = slice(128 * side, 128 * (side + 1))
        added = banded(first, window[:, lanes], side, size)
        direct = skip_gain[:, lanes] * gated[:, lanes].astype(F32)
        added = jnp.concatenate(
            [added[:8] + direct, added[8:], jnp.zeros((count - 136, 128), F32)], axis=0
        )
        gated_out[:, lanes] = (query[:, lanes] * (sums[:, lanes] + added)).astype(BF16)
    moved = None
    for part in range(2):
        term = dot(picks[part], gated_out[:, 128 * part : 128 * (part + 1)])
        moved = term if moved is None else moved + term
    outgoing[...] = moved.astype(BF16)


def pick_kernel(weights, given, kept, sems):
    core = lax.axis_index("chan") % 2
    copies = []
    for i, (lines, parity) in enumerate(((given, 1 - core), (kept, core))):
        chips, _, width = lines.shape
        for chip in range(chips):
            columns = pl.ds(pl.multiple_of((2 * chip + parity) * width, width), width)
            copies.append(pltpu.make_async_copy(weights.at[:, columns], lines.at[chip], sems.at[i, chip]))
    for copy in copies:
        copy.start()
    for copy in copies:
        copy.wait()


def out_near_kernel(packed, lines, sums):
    rows = unpack(packed, sums.shape[1])
    core = lax.axis_index("chan") % 2
    for chip in range(sums.shape[0]):
        sums[member(chip, core)] = dot(rows, lines[chip])


def out_far_kernel(packed, lines, near, sums):
    rows = unpack(packed, sums.shape[1])
    core = lax.axis_index("chan") % 2
    for chip in range(sums.shape[0]):
        place = member(chip, core)
        sums[place] = (near[place] + dot(rows, lines[chip])).astype(BF16)


def kernel(body, name, out_shape, mib, flops, moved, in_place=(), scratch=()):
    vector = pl.BlockSpec(memory_space=pltpu.VMEM)
    anywhere = pl.BlockSpec(memory_space=pltpu.HBM)

    def call(*args):
        return pl.pallas_call(
            body,
            out_shape=out_shape,
            in_specs=[anywhere if i in in_place else vector for i in range(len(args))],
            out_specs=jax.tree.map(lambda _: vector, out_shape),
            scratch_shapes=scratch,
            compiler_params=params(mib),
            cost_estimate=cost(flops, moved),
            name=name,
        )(*args)

    return call


def array(shape, dtype=BF16):
    return jax.ShapeDtypeStruct(shape, dtype)


def over_seq(packed, turn):
    chunks = packed.reshape(SEQ, 8, 128)
    order = [[device_at(chunk, turn) for chunk in range(SEQ)]]
    return lax.all_to_all(chunks, "seq", 0, 0, axis_index_groups=order, tiled=True).reshape(8 * SEQ, 128)


def body(tokens, w_in, short_filter, mr_filter, skip_gain, w_out, segments):
    rows, chans = tokens.shape
    width = w_in.shape[0]
    chan_count = lax.axis_size("chan")
    chips = chan_count // 2
    same_core = [[2 * member(place, c) + c for place in range(chips)] for c in range(2)]
    partners = [(i, i ^ 1) for i in range(chan_count)]
    holder = {int(k): d for d, k in enumerate([d // 2 if d % 2 == 0 else SEQ - 1 - d // 2 for d in range(SEQ)])}
    ahead = [(holder[k], holder[k + 1]) for k in range(SEQ - 1)]
    segments = segments.reshape(-1, 128)
    gain = skip_gain.reshape(1, chans)
    moved = rows * chans * 2

    packed = kernel(pack_kernel, "pack", array((8 * SEQ, 128)), 4, 1 << 26, 2 * moved)(tokens)
    spread = kernel(unfold_kernel, "unfold", array((chips, rows, chans)), 8, 1 << 27, 9 * moved)(over_seq(packed, TURN_IN))
    near = lax.all_to_all(spread, "chan", 0, 0, axis_index_groups=same_core, tiled=True)
    far = lax.ppermute(near, "chan", partners)
    bands = kernel(band_kernel, "bands", array((mr_filter.shape[0], 128, 256)), 8, 1 << 24, 8 * moved)(mr_filter)
    weights = w_in.transpose(1, 0, 2).reshape(3, chips, 2, chans, chans)
    lines = (3, chips, chans, chans)
    work = 3 * rows * width * chans
    partial, far_lines = kernel(
        project_near_kernel,
        "project_near",
        (array((3, rows, chans), F32), array(lines)),
        47,
        work,
        60 * moved,
        (1,),
        [pltpu.VMEM(lines, BF16), pltpu.SemaphoreType.DMA((4,))],
    )(near, weights)
    qkv, halo = kernel(
        project_far_kernel,
        "project_far",
        (array((3, rows, chans)), array((152, chans))),
        8,
        work,
        40 * moved,
    )(far, far_lines, partial, segments, short_filter)

    before = lax.ppermute(halo, "seq", ahead)
    block = array((chips, rows, chans))
    given, kept = kernel(
        pick_kernel, "pick", (block, block), 8, 0, 32 * moved, (0,), [pltpu.SemaphoreType.DMA((2, chips))]
    )(w_out)
    taken = lax.ppermute(given, "chan", partners)
    wide = array((rows, chans), F32)
    groups = mr_filter.shape[0]
    queries, own, first, edge, picks = kernel(
        mix_own_kernel,
        "mix_own",
        (wide, wide, array((groups, 136, 256)), array((16, 128), F32), array((2, 8 * SEQ, rows))),
        8,
        1 << 29,
        32 * moved,
        (),
        [pltpu.VMEM(bands.shape, BF16)],
    )(qkv, bands, segments, short_filter, gain)
    outgoing = kernel(
        mix_rest_kernel, "mix_rest", array((8 * SEQ, 128)), 8, 1 << 28, 32 * moved, (), [pltpu.VMEM((rows, chans), BF16)]
    )(qkv, before, first, edge, short_filter, gain, queries, own, picks)
    returned = over_seq(outgoing, TURN_OUT)
    other = lax.ppermute(returned, "chan", partners)
    sums = kernel(out_near_kernel, "out_near", array(block.shape, F32), 8, work // 3, 16 * moved)(returned, kept)
    sums = kernel(out_far_kernel, "out_far", block, 8, work // 3, 16 * moved)(other, taken, sums)
    terms = lax.all_to_all(sums, "chan", 0, 0, axis_index_groups=same_core, tiled=True)
    return kernel(sum_kernel, "sum", array((rows, chans)), 4, 1 << 20, 9 * moved)(terms)


def solution(mesh):
    return jax.shard_map(
        body,
        mesh=mesh,
        in_specs=(
            P("seq", "chan"),
            P(None, None, "chan"),
            P(None, None, "chan"),
            P("chan", None),
            P("chan"),
            P("chan", None),
            P(),
        ),
        out_specs=P("seq", "chan"),
        check_vma=False,
    )
```
